32 devices in a mesh: node: 4 (over y, x), space: 8 (over z, core).
Axes of the slice: x: 2, y: 2, z: 4, core: 2. Of those that a mesh axis runs over, the one named last changes fastest.
Arguments:
- start: float32 [4, 32, 64, 256], P(None, 'space'), may hold values from -6 to 6
- guess: float32 [4, 4, 32, 64, 256], P('node', None, 'space'), may hold values from -6 to 6
- heat_mask: int32 [32, 64, 256], P('space'), may hold values 0 or 1
- solid_mask: int32 [32, 64, 256], P('space'), may hold values 0 or 1
Outputs:
- iterate: float32 [4, 4, 32, 64, 256], P('node', None, 'space')
The draws below stay inside these ranges and needn't reach their ends.
All inputs are finite; a program needn't handle non-finite values. No bound on the sum of `heat_mask` or of `solid_mask` on one device may be relied on, other than what follows from the above.
Results may differ from the reference program's by a relative error of at most 0.0001.
Values sent between devices are 32-bit elements; how exact they have to be, the bound alone decides.
No kernel may reach another device: no remote copies, remote signals or barrier semaphores. Data moves between devices by JAX's collectives and lax.ppermute only.
A program may use at most 64 MiB of HBM per device.

```python
import jax
import jax.numpy as jnp
from jax import lax

NZ = 64
NY = 256
SWEEPS = 2
JACOBI = 3
NODES = 4
NX = 32


def with_ends(entries, own_key, smallest, top_value):
    longest = entries.shape.index(max(entries.shape))
    spots = []
    for shift in (0, 1):
        where = [jax.random.randint(jax.random.fold_in(own_key, axis), (), 0, length) for axis, length in enumerate(entries.shape)]
        where[longest] = (where[longest] + shift) % entries.shape[longest]
        spots.append(tuple(where))
    return entries.at[spots[0]].set(smallest).at[spots[1]].set(top_value)


def level_of(key, extent, split, low, largest):
    factor_of, own = 1.0, jax.random.fold_in(key, 6)
    for axis_at, parts in split:
        draws = jnp.exp(jax.random.uniform(jax.random.fold_in(own, axis_at), (parts,), jnp.float32, low / len(split), largest / len(split)))
        factor_of = factor_of * jnp.repeat(draws, extent[axis_at] // parts).reshape([-1 if axis == axis_at else 1 for axis in range(len(extent))])
    return factor_of


def noise(rng, dims, width, reach, pieces=(), kind=jnp.bfloat16):
    result = jax.random.normal(rng, dims, jnp.float32) * width
    if len(pieces) > 0:
        result = level_of(rng, dims, pieces, -0.22, 0.18) * result
    return jnp.clip(result, min=-reach, max=reach).astype(kind)


def setup_inputs(seed: int = 0) -> dict:
    arg_keys = jax.random.split(jax.random.key(seed), 5)
    start = noise(arg_keys[0], (4, NX, NZ, NY), 1.0, 6.0, ((1, 8),), jnp.float32)
    guess = noise(arg_keys[1], (NODES, 4, NX, NZ, NY), 1.0, 6.0, ((0, 4), (2, 8)), jnp.float32)
    heat_mask = with_ends((jax.random.randint(arg_keys[2], (NX, NZ, NY), 0, 4) < 1).astype(jnp.int32), jax.random.fold_in(arg_keys[2], 1), 0, 1)
    solid_mask = with_ends((jax.random.randint(arg_keys[3], (NX, NZ, NY), 0, 5) < 1).astype(jnp.int32), jax.random.fold_in(arg_keys[3], 1), 0, 1)
    return dict(start=start, guess=guess, heat_mask=heat_mask, solid_mask=solid_mask)


advect_rate = 0.25
buoyancy = 0.5
heating = 1.0
diffusion = (0.5, 0.5, 0.5, 0.35)


def legendre_value(order, place):
    previous = 1.0
    current = place
    if order == 0:
        return previous
    for degree in range(1, order):
        following = ((2 * degree + 1) * place * current - degree * previous) / (degree + 1)
        previous = current
        current = following
    return current


def radau_tables(count):
    def radau_poly(place):
        return legendre_value(count, place) - legendre_value(count - 1, place)

    samples = 4000 * count
    roots_found = []
    left_end = -1.0
    left_value = radau_poly(left_end)
    for index in range(1, samples + 1):
        right_end = -1.0 + (2.0 - 1e-7) * index / samples
        right_value = radau_poly(right_end)
        if left_value * right_value < 0.0:
            low_end = left_end
            high_end = right_end
            low_value = left_value
            for repeat in range(200):
                middle = 0.5 * (low_end + high_end)
                middle_value = radau_poly(middle)
                if low_value * middle_value <= 0.0:
                    high_end = middle
                else:
                    low_end = middle
                    low_value = middle_value
            roots_found.append(0.5 * (low_end + high_end))
        left_end = right_end
        left_value = right_value
    points = [(value + 1.0) / 2.0 for value in roots_found[:count - 1]] + [1.0]
    table = []
    for row in range(count):
        table.append([0.0] * count)
    for column in range(count):
        coefficients = [1.0]
        for other in range(count):
            if other == column:
                continue
            scale = 1.0 / (points[column] - points[other])
            widened = [0.0] * (len(coefficients) + 1)
            for index in range(len(coefficients)):
                widened[index + 1] += coefficients[index] * scale
                widened[index] -= points[other] * coefficients[index] * scale
            coefficients = widened
        for row in range(count):
            total = 0.0
            for index in range(len(coefficients)):
                total += coefficients[index] * points[row] ** (index + 1) / (index + 1)
            table[row][column] = total
    return points, table


def shifted(field, axis, offset):
    length = field.shape[axis]
    zero_shape = list(field.shape)
    zero_shape[axis] = abs(offset)
    zeros = jnp.zeros(zero_shape, field.dtype)
    if offset > 0:
        kept = lax.slice_in_dim(field, offset, length, axis=axis)
        return jnp.concatenate([kept, zeros], axis)
    kept = lax.slice_in_dim(field, 0, length + offset, axis=axis)
    return jnp.concatenate([zeros, kept], axis)


def neighbour_sum(padded):
    centre = padded[:, 1:-1]
    total = padded[:, 2:] + padded[:, :-2]
    total = total + shifted(centre, 2, 1) + shifted(centre, 2, -1)
    total = total + shifted(centre, 3, 1) + shifted(centre, 3, -1)
    return total


def tendency(padded, heat_mask, solid_mask):
    centre = padded[:, 1:-1]
    grad_x = (padded[:, 2:] - padded[:, :-2]) * 0.5
    grad_z = (shifted(centre, 2, 1) - shifted(centre, 2, -1)) * 0.5
    grad_y = (shifted(centre, 3, 1) - shifted(centre, 3, -1)) * 0.5
    transport = centre[0:1] * grad_x + centre[1:2] * grad_y + centre[2:3] * grad_z
    rates = jnp.asarray(diffusion, jnp.float32).reshape(4, 1, 1, 1)
    diffusive = rates * (neighbour_sum(padded) - 6.0 * centre)
    blank = jnp.zeros_like(centre[3])
    source = jnp.stack([blank, blank, buoyancy * centre[3], heating * heat_mask.astype(jnp.float32)])
    fluid = 1.0 - solid_mask.astype(jnp.float32)
    keeper = jnp.stack([fluid, fluid, fluid, jnp.ones_like(fluid)])
    total = (-advect_rate * transport + diffusive + source) * keeper
    return total, diffusive


def pad_x(field):
    return jnp.pad(field, ((0, 0), (1, 1), (0, 0), (0, 0)))


def reference(start, guess, heat_mask, solid_mask):
    points_list, table_list = radau_tables(NODES)
    table = jnp.asarray(table_list, jnp.float32)
    points = jnp.asarray(points_list, jnp.float32)
    rates = jnp.asarray(diffusion, jnp.float32).reshape(4, 1, 1, 1)
    iterate = guess
    for sweep in range(SWEEPS):
        pairs = [tendency(pad_x(iterate[node]), heat_mask, solid_mask) for node in range(NODES)]
        stacked = jnp.stack([pair[0] for pair in pairs])
        summed = jnp.einsum('mj,jabcd->mabcd', table, stacked, precision=lax.Precision.HIGHEST)
        updated = []
        for node in range(NODES):
            point = points[node]
            coupling = point * rates
            right = start + summed[node] - point * pairs[node][1]
            current = iterate[node]
            for level in range(JACOBI):
                current = (right + coupling * neighbour_sum(pad_x(current))) / (1.0 + 6.0 * coupling)
            updated.append(current)
        iterate = jnp.stack(updated)
    return iterate
```

```python
import functools

import jax
import jax.numpy as jnp
import numpy as np
from jax import lax
from jax.experimental import pallas as pl
from jax.experimental.pallas import tpu as pltpu
from jax.sharding import PartitionSpec as P

SWEEPS = 2
JACOBI = 3
LANES = 128
VMEM_LIMIT = 56 << 20

advect_rate = 0.25
buoyancy = 0.5
heating = 1.0
diffusion = (0.5, 0.5, 0.5, 0.35)


def legendre_value(order, place):
    previous = 1.0
    current = place
    for degree in range(1, order):
        following = ((2 * degree + 1) * place * current - degree * previous) / (degree + 1)
        previous = current
        current = following
    return current


def radau_tables(count):

    def radau_poly(place):
        return legendre_value(count, place) - legendre_value(count - 1, place)

    samples = 4000 * count
    roots_found = []
    left_end = -1.0
    left_value = radau_poly(left_end)
    for index in range(1, samples + 1):
        right_end = -1.0 + (2.0 - 1e-07) * index / samples
        right_value = radau_poly(right_end)
        if left_value * right_value < 0.0:
            low_end = left_end
            high_end = right_end
            low_value = left_value
            for repeat in range(200):
                middle = 0.5 * (low_end + high_end)
                middle_value = radau_poly(middle)
                if low_value * middle_value <= 0.0:
                    high_end = middle
                else:
                    low_end = middle
                    low_value = middle_value
            roots_found.append(0.5 * (low_end + high_end))
        left_end = right_end
        left_value = right_value
    points = [(value + 1.0) / 2.0 for value in roots_found[: count - 1]] + [1.0]
    table = []
    for row in range(count):
        table.append([0.0] * count)
    for column in range(count):
        coefficients = [1.0]
        for other in range(count):
            if other == column:
                continue
            scale = 1.0 / (points[column] - points[other])
            widened = [0.0] * (len(coefficients) + 1)
            for index in range(len(coefficients)):
                widened[index + 1] += coefficients[index] * scale
                widened[index] -= points[other] * coefficients[index] * scale
            coefficients = widened
        for row in range(count):
            total = 0.0
            for index in range(len(coefficients)):
                total += coefficients[index] * points[row] ** (index + 1) / (index + 1)
            table[row][column] = total
    return (points, table)


def round_up(value, step):
    return -(-value // step) * step


class Geometry:
    def __init__(self, nodes, planes, depth):
        overlap = SWEEPS * JACOBI if nodes > 1 else 0
        self.nodes, self.planes, self.depth = nodes, planes, depth
        self.window = -(-(depth + 2 * overlap * (nodes - 1)) // nodes)
        step = self.window - 2 * overlap
        assert step > 0 and planes >= JACOBI
        self.offset = [min(p * step, depth - self.window) for p in range(nodes)]
        first = [0] + [p * step + overlap for p in range(1, nodes)]
        last = first[1:] + [depth]
        self.first, self.count = first, [b - a for a, b in zip(first, last)]
        self.stride = self.window + 1
        while (planes * self.stride) % 8:
            self.stride += 1
        self.rows = planes * self.stride
        self.side = round_up(JACOBI * self.stride, 8)
        self.aux_side = round_up((JACOBI - 1) * self.stride, 8)
        self.low = 8 + self.side
        self.total = self.low + self.rows + self.side + 8
        self.back = max(self.count)
        while (planes * self.back) % 8:
            self.back += 1

    def span(self, reach):
        begin = (self.low - reach * self.stride) // 8 * 8
        end = round_up(self.low + (self.planes + reach) * self.stride, 8)
        assert begin - self.stride >= 0 and end + self.stride <= self.total
        return begin, end


def pack_kernel(geo, guess_ref, out_ref):
    blank = jnp.zeros((geo.stride - geo.window, LANES), jnp.float32)
    for p in range(geo.nodes):
        for f in range(4):
            for x in range(geo.planes):
                for h in range(2):
                    at = x * geo.stride
                    out_ref[p, f, h, at : at + geo.window] = guess_ref[
                        0, f, x, geo.offset[p] : geo.offset[p] + geo.window, h * LANES : (h + 1) * LANES
                    ]
                    out_ref[p, f, h, at + geo.window : at + geo.stride] = blank


def pack_aux_kernel(geo, me_ref, start_ref, heat_ref, solid_ref, out_ref):
    blank = jnp.zeros((geo.stride - geo.window, LANES), jnp.float32)
    me = me_ref[0]
    for p in range(geo.nodes):

        @pl.when(me == p)
        def _():
            rows = slice(geo.offset[p], geo.offset[p] + geo.window)
            for x in range(geo.planes):
                for h in range(2):
                    at = x * geo.stride
                    lanes = slice(h * LANES, (h + 1) * LANES)
                    for f in range(4):
                        out_ref[f, h, at : at + geo.window] = start_ref[f, x, rows, lanes]
                    out_ref[4, h, at : at + geo.window] = heating * heat_ref[x, rows, lanes].astype(jnp.float32)
                    out_ref[5, h, at : at + geo.window] = 1.0 - solid_ref[x, rows, lanes].astype(jnp.float32)
                    for f in range(6):
                        out_ref[f, h, at + geo.window : at + geo.stride] = blank


def sweep_kernel(
    geo, last, points, table, me_ref, coef_ref, own_ref, lo_ref, hi_ref, aux_ref, auxlo_ref, auxhi_ref, mask_ref, out_ref,
    field, tend, first, base, aux, sems,
):
    n, stride, low = geo.nodes, geo.stride, geo.low
    copies = [
        pltpu.make_async_copy(own_ref, field.at[:, :, :, pl.ds(low, geo.rows)], sems.at[0]),
        pltpu.make_async_copy(lo_ref, field.at[:, :, :, pl.ds(low - geo.side, geo.side)], sems.at[1]),
        pltpu.make_async_copy(hi_ref, field.at[:, :, :, pl.ds(low + geo.rows, geo.side)], sems.at[2]),
        pltpu.make_async_copy(aux_ref, aux.at[:, :, pl.ds(low, geo.rows)], sems.at[3]),
        pltpu.make_async_copy(auxlo_ref, aux.at[:, :, pl.ds(low - geo.aux_side, geo.aux_side)], sems.at[4]),
        pltpu.make_async_copy(auxhi_ref, aux.at[:, :, pl.ds(low + geo.rows, geo.aux_side)], sems.at[5]),
    ]
    for copy in copies:
        copy.start()
    lane = lax.broadcasted_iota(jnp.int32, (8, LANES), 1)
    is_first, is_last = lane == 0, lane == LANES - 1
    for copy in copies:
        copy.wait()

    def sides(a, b):
        ra, rb = pltpu.roll(a, 1, 1), pltpu.roll(b, 1, 1)
        la, lb = pltpu.roll(a, LANES - 1, 1), pltpu.roll(b, LANES - 1, 1)
        minus = (jnp.where(is_first, 0.0, ra), jnp.where(is_first, ra, rb))
        plus = (jnp.where(is_last, lb, la), jnp.where(is_last, 0.0, lb))
        return minus, plus

    begin, end = geo.span(JACOBI - 1)

    def node_tendency(j, _):
        for r in range(begin, end, 8):
            rows = pl.ds(r, 8)
            vel = []
            for h in range(2):
                vel.append([(-0.5 * advect_rate) * field[j, f, h, rows] for f in range(3)])
            for f in range(4):
                centre = [field[j, f, h, rows] for h in range(2)]
                minus, plus = sides(centre[0], centre[1])
                for h in range(2):
                    xp, xm = field[j, f, h, pl.ds(r + stride, 8)], field[j, f, h, pl.ds(r - stride, 8)]
                    zp, zm = field[j, f, h, pl.ds(r + 1, 8)], field[j, f, h, pl.ds(r - 1, 8)]
                    near = (xp + xm) + (zp + zm) + (plus[h] + minus[h])
                    moved = vel[h][0] * (xp - xm) + vel[h][1] * (plus[h] - minus[h]) + vel[h][2] * (zp - zm)
                    total = moved + diffusion[f] * (near - 6.0 * centre[h])
                    if f == 2:
                        total = total + buoyancy * field[j, 3, h, rows]
                    if f == 3:
                        total = total + aux[4, h, rows]
                    else:
                        total = total * aux[5, h, rows]
                    tend[j, f, h, rows] = total
                    base[j, f, h, rows] = near
        return 0

    lax.fori_loop(0, n, node_tendency, 0)

    def quadrature(t, _):
        rows = pl.ds(pl.multiple_of(begin + t * 8, 8), 8)
        mask = mask_ref[rows]
        for f in range(4):
            scale = [mask * (1.0 / (1.0 + 6.0 * points[m] * diffusion[f])) for m in range(n)]
            for h in range(2):
                slopes = [tend[j, f, h, rows] for j in range(n)]
                begun = aux[f, h, rows]
                for m in range(n):
                    c = points[m] * diffusion[f]
                    total = begun + (6.0 * c) * field[m, f, h, rows]
                    for j in range(n):
                        total = total + table[m][j] * slopes[j]
                    total = total * scale[m]
                    first[m, f, h, rows] = total
                    base[m, f, h, rows] = total - (c * scale[m]) * base[m, f, h, rows]
        return 0

    lax.fori_loop(0, (end - begin) // 8, quadrature, 0)

    def relax(source, target, reach, shift):
        rbegin, rend = geo.span(reach)

        def channel(k, _):
            m, f = k // 4, k % 4
            weight = coef_ref[k]
            for r in range(rbegin, rend, 8):
                rows = pl.ds(r, 8)
                mask = mask_ref[rows] * weight
                minus, plus = sides(source[m, f, 0, rows], source[m, f, 1, rows])
                for h in range(2):
                    near = (
                        (source[m, f, h, pl.ds(r + stride, 8)] + source[m, f, h, pl.ds(r - stride, 8)])
                        + (source[m, f, h, pl.ds(r + 1, 8)] + source[m, f, h, pl.ds(r - 1, 8)])
                        + (plus[h] + minus[h])
                    )
                    target[m, f, h, pl.ds(r - shift, 8)] = base[m, f, h, rows] + mask * near
            return 0

        lax.fori_loop(0, 4 * n, channel, 0)

    relax(first, tend, 1, 0)
    if not last:
        relax(tend, out_ref, 0, low)
        return
    relax(tend, first, 0, 0)
    me = me_ref[0]
    for start in sorted({a - b for a, b in zip(geo.first, geo.offset)}):
        hit = [p for p in range(n) if geo.first[p] - geo.offset[p] == start]
        chosen = functools.reduce(jnp.logical_or, [me == p for p in hit])
        count = min(geo.back, geo.stride - start)

        @pl.when(chosen)
        def _():
            def channel(k, _):
                m, f = k // 4, k % 4
                for h in range(2):
                    for x in range(geo.planes):
                        out_ref[m, f, h, x * geo.back : x * geo.back + count] = first[
                            m, f, h, low + x * stride + start : low + x * stride + start + count
                        ]
                return 0

            lax.fori_loop(0, 4 * n, channel, 0)


def unpack_kernel(geo, in_ref, out_ref):
    for p in range(geo.nodes):
        for f in range(4):
            for x in range(geo.planes):
                for h in range(2):
                    at = x * geo.back
                    out_ref[0, f, x, geo.first[p] : geo.first[p] + geo.count[p], h * LANES : (h + 1) * LANES] = in_ref[
                        p, f, h, at : at + geo.count[p]
                    ]


def on_device(start, guess, heat_mask, solid_mask):
    n = lax.axis_size("node")
    tiles = lax.axis_size("space")
    planes, depth, width = guess.shape[2:]
    assert width == 2 * LANES
    geo = Geometry(n, planes, depth)
    points_list, table_list = radau_tables(n)
    table = [[float(np.float32(v)) for v in row] for row in table_list]
    points = [float(np.float32(v)) for v in points_list]
    me = lax.axis_index("node").reshape(1).astype(jnp.int32)
    tile = lax.axis_index("space")
    up = [(i, i + 1) for i in range(tiles - 1)]
    down = [(i + 1, i) for i in range(tiles - 1)]
    params = pltpu.CompilerParams(vmem_limit_bytes=VMEM_LIMIT)
    vmem, smem, anywhere = (
        pl.BlockSpec(memory_space=pltpu.VMEM), pl.BlockSpec(memory_space=pltpu.SMEM), pl.BlockSpec(memory_space=pl.ANY)
    )
    f32 = jnp.float32

    packed = pl.pallas_call(
        functools.partial(pack_kernel, geo), name="pack",
        out_shape=jax.ShapeDtypeStruct((n, 4, 2, geo.rows, LANES), f32),
        in_specs=[vmem], out_specs=vmem, compiler_params=params,
    )(guess)
    aux = pl.pallas_call(
        functools.partial(pack_aux_kernel, geo), name="pack_aux",
        out_shape=jax.ShapeDtypeStruct((6, 2, geo.rows, LANES), f32),
        in_specs=[smem, vmem, vmem, vmem], out_specs=vmem, compiler_params=params,
    )(me, start, heat_mask, solid_mask)
    aux_lo = lax.ppermute(aux[:, :, geo.rows - geo.aux_side :], "space", up)
    aux_hi = lax.ppermute(aux[:, :, : geo.aux_side], "space", down)

    row = np.arange(geo.total) - geo.low
    inside = (row % geo.stride) < geo.window
    plane = row // geo.stride + tile * planes
    mask = jnp.where(inside & (plane >= 0) & (plane < planes * tiles), 1.0, 0.0).astype(f32)
    mask = jnp.broadcast_to(mask[:, None], (geo.total, LANES))
    coef = jnp.asarray(
        [points[m] * d / (1.0 + 6.0 * points[m] * d) for m in range(n) for d in diffusion], f32
    )

    own = lax.all_to_all(packed, "node", split_axis=0, concat_axis=0, tiled=True)
    for sweep in range(SWEEPS):
        last = sweep == SWEEPS - 1
        lo = lax.ppermute(own[:, :, :, geo.rows - geo.side :], "space", up)
        hi = lax.ppermute(own[:, :, :, : geo.side], "space", down)
        rows = planes * geo.back if last else geo.rows
        big = pltpu.VMEM((n, 4, 2, geo.total, LANES), f32)
        own = pl.pallas_call(
            functools.partial(sweep_kernel, geo, last, points, table), name="sweep",
            out_shape=jax.ShapeDtypeStruct((n, 4, 2, rows, LANES), f32),
            in_specs=[smem, smem, anywhere, anywhere, anywhere, anywhere, anywhere, anywhere, vmem], out_specs=vmem,
            scratch_shapes=[big, big, big, big, pltpu.VMEM((6, 2, geo.total, LANES), f32), pltpu.SemaphoreType.DMA((6,))],
            compiler_params=params,
        )(me, coef, own, lo, hi, aux, aux_lo, aux_hi, mask)
    back = lax.all_to_all(own, "node", split_axis=0, concat_axis=0, tiled=True)
    return pl.pallas_call(
        functools.partial(unpack_kernel, geo), name="unpack",
        out_shape=jax.ShapeDtypeStruct((1, 4, planes, depth, width), f32),
        in_specs=[vmem], out_specs=vmem, compiler_params=params,
    )(back)


def solution(mesh):
    in_specs = (
        P(None, "space", None, None),
        P("node", None, "space", None, None),
        P("space", None, None),
        P("space", None, None),
    )
    out_specs = P("node", None, "space", None, None)
    return jax.shard_map(
        on_device, mesh=mesh, in_specs=in_specs, out_specs=out_specs, check_vma=False
    )
```

```python
import functools

import jax
import jax.numpy as jnp
import numpy as np
from jax import lax
from jax.experimental import pallas as pl
from jax.experimental.pallas import tpu as pltpu
from jax.sharding import PartitionSpec as P

SWEEPS = 2
JACOBI = 3
LANES = 128
VMEM_LIMIT = 56 << 20

advect_rate = 0.25
buoyancy = 0.5
heating = 1.0
diffusion = (0.5, 0.5, 0.5, 0.35)


def legendre_value(order, place):
    previous = 1.0
    current = place
    for degree in range(1, order):
        following = ((2 * degree + 1) * place * current - degree * previous) / (degree + 1)
        previous = current
        current = following
    return current


def radau_tables(count):

    def radau_poly(place):
        return legendre_value(count, place) - legendre_value(count - 1, place)

    samples = 4000 * count
    roots_found = []
    left_end = -1.0
    left_value = radau_poly(left_end)
    for index in range(1, samples + 1):
        right_end = -1.0 + (2.0 - 1e-07) * index / samples
        right_value = radau_poly(right_end)
        if left_value * right_value < 0.0:
            low_end = left_end
            high_end = right_end
            low_value = left_value
            for repeat in range(200):
                middle = 0.5 * (low_end + high_end)
                middle_value = radau_poly(middle)
                if low_value * middle_value <= 0.0:
                    high_end = middle
                else:
                    low_end = middle
                    low_value = middle_value
            roots_found.append(0.5 * (low_end + high_end))
        left_end = right_end
        left_value = right_value
    points = [(value + 1.0) / 2.0 for value in roots_found[: count - 1]] + [1.0]
    table = []
    for row in range(count):
        table.append([0.0] * count)
    for column in range(count):
        coefficients = [1.0]
        for other in range(count):
            if other == column:
                continue
            scale = 1.0 / (points[column] - points[other])
            widened = [0.0] * (len(coefficients) + 1)
            for index in range(len(coefficients)):
                widened[index + 1] += coefficients[index] * scale
                widened[index] -= points[other] * coefficients[index] * scale
            coefficients = widened
        for row in range(count):
            total = 0.0
            for index in range(len(coefficients)):
                total += coefficients[index] * points[row] ** (index + 1) / (index + 1)
            table[row][column] = total
    return (points, table)


def round_up(value, step):
    return -(-value // step) * step


class Geometry:
    def __init__(self, nodes, planes, depth):
        overlap = SWEEPS * JACOBI if nodes > 1 else 0
        self.nodes, self.planes, self.depth = nodes, planes, depth
        self.window = -(-(depth + 2 * overlap * (nodes - 1)) // nodes)
        step = self.window - 2 * overlap
        assert step > 0 and planes >= JACOBI
        self.offset = [min(p * step, depth - self.window) for p in range(nodes)]
        first = [0] + [p * step + overlap for p in range(1, nodes)]
        last = first[1:] + [depth]
        self.first, self.count = first, [b - a for a, b in zip(first, last)]
        self.stride = self.window + 1
        while (planes * self.stride) % 8:
            self.stride += 1
        self.rows = planes * self.stride
        self.side = round_up(JACOBI * self.stride, 8)
        self.low = 8 + self.side
        self.total = self.low + self.rows + self.side + 8
        self.back = max(self.count)
        while (planes * self.back) % 8:
            self.back += 1

    def span(self, reach):
        begin = (self.low - reach * self.stride) // 8 * 8
        end = round_up(self.low + (self.planes + reach) * self.stride, 8)
        assert begin - self.stride >= 0 and end + self.stride <= self.total
        return begin, end


def copy_all(pairs, sems):
    copies = [pltpu.make_async_copy(source, target, sems.at[i]) for i, (source, target) in enumerate(pairs)]
    for copy in copies:
        copy.start()
    for copy in copies:
        copy.wait()


def pack_kernel(geo, guess_ref, *refs):
    *outs, windows, sems = refs
    me = lax.axis_index("node")
    blank = jnp.zeros((geo.stride - geo.window, LANES), jnp.float32)
    for p in range(geo.nodes):
        for f in range(4):
            for x in range(geo.planes):
                for h in range(2):
                    at = x * geo.stride
                    windows[p, f, h, at : at + geo.window] = guess_ref[
                        0, f, x, geo.offset[p] : geo.offset[p] + geo.window, h * LANES : (h + 1) * LANES
                    ]
                    windows[p, f, h, at + geo.window : at + geo.stride] = blank
    copy_all([(windows.at[me ^ k], outs[k - 1]) for k in range(1, geo.nodes)], sems)


def send_rows(geo, odd):
    far = geo.rows - geo.side
    return pl.multiple_of(far * (1 - odd), 8), pl.multiple_of(far * odd, 8)


def halo_rows(geo, odd):
    below, above = geo.low - geo.side, geo.low + geo.rows
    return (
        pl.multiple_of(above + (below - above) * odd, 8),
        pl.multiple_of(below + (above - below) * odd, 8),
    )


def pack_own_kernel(
    geo, guess_ref, start_ref, heat_ref, solid_ref, own_ref, aux_ref, near_ref, far_ref, packed, sems
):
    me, odd = lax.axis_index("node"), lax.axis_index("space") % 2
    blank = jnp.zeros((geo.stride - geo.window, LANES), jnp.float32)
    for p in range(geo.nodes):

        @pl.when(me == p)
        def _():
            rows = slice(geo.offset[p], geo.offset[p] + geo.window)
            for x in range(geo.planes):
                for h in range(2):
                    at = x * geo.stride
                    lanes = slice(h * LANES, (h + 1) * LANES)
                    for f in range(4):
                        packed[f, h, at : at + geo.window] = guess_ref[0, f, x, rows, lanes]
                        packed[4 + f, h, at : at + geo.window] = start_ref[f, x, rows, lanes]
                    packed[8, h, at : at + geo.window] = heating * heat_ref[x, rows, lanes].astype(jnp.float32)
                    packed[9, h, at : at + geo.window] = 1.0 - solid_ref[x, rows, lanes].astype(jnp.float32)
                    for f in range(10):
                        packed[f, h, at + geo.window : at + geo.stride] = blank

    near, far = send_rows(geo, odd)
    copy_all(
        [
            (packed.at[:, :, pl.ds(far, geo.side)], far_ref),
            (packed.at[:, :, pl.ds(near, geo.side)], near_ref),
            (packed.at[pl.ds(0, 4)], own_ref),
            (packed.at[pl.ds(4, 6)], aux_ref),
        ],
        sems,
    )


def pick(index, values):
    chosen = jnp.float32(values[-1])
    for i in reversed(range(len(values) - 1)):
        chosen = jnp.where(index == i, jnp.float32(values[i]), chosen)
    return chosen


def sweep_kernel(geo, opening, tiles, points, table, aux_ref, near0_ref, far0_ref, *refs):
    n, stride, low, side = geo.nodes, geo.stride, geo.low, geo.side
    me, tile = lax.axis_index("node"), lax.axis_index("space")
    odd = tile % 2
    *refs, field, tend, first, base, aux, mask, sems = refs
    near, far = halo_rows(geo, odd)
    near_from, far_from = send_rows(geo, 1 - odd)
    own_rows, near_rows, far_rows = pl.ds(low, geo.rows), pl.ds(near, side), pl.ds(far, side)
    pairs = [
        (aux_ref, aux.at[:, :, own_rows]),
        (near0_ref.at[pl.ds(4, 6)], aux.at[:, :, near_rows]),
        (far0_ref.at[pl.ds(4, 6)], aux.at[:, :, far_rows]),
    ]
    for k in range(n):
        j = me ^ k if opening else k
        if opening and k == 0:
            sources = refs[0], near0_ref.at[pl.ds(0, 4)], far0_ref.at[pl.ds(0, 4)]
        elif opening:
            own_ref, near_ref, far_ref = refs[3 * k - 2 : 3 * k + 1]
            sources = own_ref, near_ref.at[:, :, pl.ds(near_from, side)], far_ref.at[:, :, pl.ds(far_from, side)]
        else:
            sources = [ref.at[k] for ref in refs[:3]]
        pairs += zip(sources, [field.at[j, :, :, rows] for rows in (own_rows, near_rows, far_rows)])
    copies = [pltpu.make_async_copy(source, target, sems.at[i]) for i, (source, target) in enumerate(pairs)]
    for copy in copies:
        copy.start()
    refs = refs[3 * n - 2 :] if opening else refs[3:]

    mask[...] = jnp.zeros(mask.shape, jnp.float32)
    for q in range(-JACOBI, geo.planes + JACOBI):
        there = jnp.float32(1.0)
        if q < 0:
            there = jnp.where(tile > 0, 1.0, 0.0)
        if q >= geo.planes:
            there = jnp.where(tile < tiles - 1, 1.0, 0.0)
        mask[low + q * stride : low + q * stride + geo.window] = jnp.full((geo.window, LANES), there, jnp.float32)
    lane = lax.broadcasted_iota(jnp.int32, (8, LANES), 1)
    is_first, is_last = lane == 0, lane == LANES - 1
    for copy in copies[:3]:
        copy.wait()

    def sides(a, b):
        ra, rb = pltpu.roll(a, 1, 1), pltpu.roll(b, 1, 1)
        la, lb = pltpu.roll(a, LANES - 1, 1), pltpu.roll(b, LANES - 1, 1)
        minus = (jnp.where(is_first, 0.0, ra), jnp.where(is_first, ra, rb))
        plus = (jnp.where(is_last, lb, la), jnp.where(is_last, 0.0, lb))
        return minus, plus

    begin, end = geo.span(JACOBI - 1)

    def node_tendency(k, _):
        j = me ^ k if opening else k
        for i, rows in enumerate((own_rows, near_rows, far_rows)):
            part = field.at[j, :, :, rows]
            pltpu.make_async_copy(part, part, sems.at[3 + 3 * k + i]).wait()
        for r in range(begin, end, 8):
            rows = pl.ds(r, 8)
            vel = []
            for h in range(2):
                vel.append([(-0.5 * advect_rate) * field[j, f, h, rows] for f in range(3)])
            for f in range(4):
                centre = [field[j, f, h, rows] for h in range(2)]
                minus, plus = sides(centre[0], centre[1])
                for h in range(2):
                    xp, xm = field[j, f, h, pl.ds(r + stride, 8)], field[j, f, h, pl.ds(r - stride, 8)]
                    zp, zm = field[j, f, h, pl.ds(r + 1, 8)], field[j, f, h, pl.ds(r - 1, 8)]
                    near = (xp + xm) + (zp + zm) + (plus[h] + minus[h])
                    moved = vel[h][0] * (xp - xm) + vel[h][1] * (plus[h] - minus[h]) + vel[h][2] * (zp - zm)
                    total = moved + diffusion[f] * (near - 6.0 * centre[h])
                    if f == 2:
                        total = total + buoyancy * field[j, 3, h, rows]
                    if f == 3:
                        total = total + aux[4, h, rows]
                    else:
                        total = total * aux[5, h, rows]
                    tend[j, f, h, rows] = total
                    base[j, f, h, rows] = near
        return 0

    lax.fori_loop(0, n, node_tendency, 0)

    def quadrature(t, _):
        rows = pl.ds(pl.multiple_of(begin + t * 8, 8), 8)
        inside = mask[rows]
        for f in range(4):
            scale = [inside * (1.0 / (1.0 + 6.0 * points[m] * diffusion[f])) for m in range(n)]
            for h in range(2):
                slopes = [tend[j, f, h, rows] for j in range(n)]
                begun = aux[f, h, rows]
                for m in range(n):
                    c = points[m] * diffusion[f]
                    total = begun + (6.0 * c) * field[m, f, h, rows]
                    for j in range(n):
                        total = total + table[m][j] * slopes[j]
                    total = total * scale[m]
                    first[m, f, h, rows] = total
                    base[m, f, h, rows] = total - (c * scale[m]) * base[m, f, h, rows]
        return 0

    lax.fori_loop(0, (end - begin) // 8, quadrature, 0)

    def weights(m):
        return [pick(m, [p * d / (1.0 + 6.0 * p * d) for p in points]) for d in diffusion]

    def relax_rows(source, target, m, f, r, weight, to):
        minus, plus = sides(source[m, f, 0, pl.ds(r, 8)], source[m, f, 1, pl.ds(r, 8)])
        for h in range(2):
            near = (
                (source[m, f, h, pl.ds(r + stride, 8)] + source[m, f, h, pl.ds(r - stride, 8)])
                + (source[m, f, h, pl.ds(r + 1, 8)] + source[m, f, h, pl.ds(r - 1, 8)])
                + (plus[h] + minus[h])
            )
            target[m, f, h, pl.ds(to, 8)] = base[m, f, h, pl.ds(r, 8)] + weight * near

    def relax(source, target, m, reach):
        weight = weights(m)
        for r in range(*geo.span(reach), 8):
            inside = mask[pl.ds(r, 8)]
            for f in range(4):
                relax_rows(source, target, m, f, r, inside * weight[f], r)

    def relax_second(m, _):
        relax(first, tend, m, 1)
        return 0

    lax.fori_loop(0, n, relax_second, 0)

    if opening:
        out_ref, near_ref, far_ref = refs
        near, far = send_rows(geo, odd)

        def results(m, start):
            for i, (row, count, ref) in enumerate(((far, side, far_ref), (near, side, near_ref), (0, geo.rows, out_ref))):
                part = first.at[m, :, :, pl.ds(pl.multiple_of(low + row, 8), count)]
                copy = pltpu.make_async_copy(part, ref.at[m], sems.at[3 + 3 * m + i])
                copy.start() if start else copy.wait()

        def relax_third(m, _):
            relax(tend, first, m, 0)
            results(m, True)
            return 0

        lax.fori_loop(0, n, relax_third, 0)
        for m in range(n):
            results(m, False)
        return

    done = pl.ds(0, geo.planes * geo.back)
    for start in sorted({a - b for a, b in zip(geo.first, geo.offset)}):
        hit = [p for p in range(n) if geo.first[p] - geo.offset[p] == start]
        chosen = functools.reduce(jnp.logical_or, [me == p for p in hit])

        @pl.when(chosen)
        def _():
            def relax_third(i, _):
                k = n - 1 - i
                m = me ^ k
                weight = weights(m)
                for x in range(geo.planes):
                    for o in [*range(0, geo.back - 8, 8), geo.back - 8]:
                        for f in range(4):
                            relax_rows(tend, first, m, f, low + x * stride + start + o, weight[f], x * geo.back + o)
                for other in range(n):

                    @pl.when(k == other)
                    def _():
                        pltpu.make_async_copy(first.at[m, :, :, done], refs[other], sems.at[other]).start()

                return 0

            lax.fori_loop(0, n, relax_third, 0)

    for k in range(n):
        pltpu.make_async_copy(first.at[me ^ k, :, :, done], refs[k], sems.at[k]).wait()


def unpack_kernel(geo, *refs):
    ins, (out_ref, pieces, sems) = refs[: geo.nodes], refs[geo.nodes :]
    me = lax.axis_index("node")
    copy_all([(ins[k], pieces.at[me ^ k]) for k in range(geo.nodes)], sems)
    for p in range(geo.nodes):
        for f in range(4):
            for x in range(geo.planes):
                for h in range(2):
                    at = x * geo.back
                    out_ref[0, f, x, geo.first[p] : geo.first[p] + geo.count[p], h * LANES : (h + 1) * LANES] = pieces[
                        p, f, h, at : at + geo.count[p]
                    ]


def on_device(start, guess, heat_mask, solid_mask):
    n = lax.axis_size("node")
    tiles = lax.axis_size("space")
    planes, depth, width = guess.shape[2:]
    assert width == 2 * LANES and tiles % 2 == 0 and n & (n - 1) == 0
    geo = Geometry(n, planes, depth)
    points_list, table_list = radau_tables(n)
    table = [[float(np.float32(v)) for v in row] for row in table_list]
    points = [float(np.float32(v)) for v in points_list]
    f32 = jnp.float32
    vmem, hbm = pl.BlockSpec(memory_space=pltpu.VMEM), pl.BlockSpec(memory_space=pltpu.HBM)

    def call(kernel, name, outs, ins, spec, out_spec, scratch, copies):
        return pl.pallas_call(
            kernel, name=name,
            out_shape=[jax.ShapeDtypeStruct(shape, f32) for shape in outs],
            in_specs=[spec] * len(ins), out_specs=[out_spec] * len(outs),
            scratch_shapes=[pltpu.VMEM(shape, f32) for shape in scratch] + [pltpu.SemaphoreType.DMA((copies,))],
            compiler_params=pltpu.CompilerParams(vmem_limit_bytes=VMEM_LIMIT),
        )(*ins)

    def across(k, value):
        return lax.ppermute(value, "node", [(i, i ^ k) for i in range(n)])

    chip = [(i, i ^ 1) for i in range(tiles)]
    links = [(i, i + 1) for i in range(1, tiles - 1, 2)] + [(i + 1, i) for i in range(1, tiles - 1, 2)]

    def beside(near, far):
        return lax.ppermute(near, "space", chip), lax.ppermute(far, "space", links)

    piece = (4, 2, geo.rows, LANES)
    sends = call(
        functools.partial(pack_kernel, geo), "pack", [piece] * (n - 1), (guess,), vmem, hbm, [(n,) + piece], n - 1
    )
    edge = (10, 2, geo.side, LANES)
    own, aux, near, far = call(
        functools.partial(pack_own_kernel, geo), "pack_own", [piece, (6,) + piece[1:], edge, edge],
        (guess, start, heat_mask, solid_mask), vmem, hbm, [(10,) + piece[1:]], 4,
    )
    near0, far0 = beside(near, far)

    owns = {0: own}
    wave = []
    for hops in range(1, n.bit_length()):
        group = [k for k in range(1, n) if k.bit_count() == hops]
        gated = lax.optimization_barrier([sends[k - 1] for k in group] + wave)
        wave = [across(k, value) for k, value in zip(group, gated)]
        owns.update(zip(group, wave))
    pieces = [own]
    for k in range(1, n):
        pieces += [owns[k], *beside(owns[k], owns[k])]

    big = (n, 4, 2, geo.total, LANES)
    scratch = [big, big, big, big, (6, 2, geo.total, LANES), (geo.total, LANES)]
    edge = (n, 4, 2, geo.side, LANES)
    own, near, far = call(
        functools.partial(sweep_kernel, geo, True, tiles, points, table), "sweep_opening", [(n,) + piece, edge, edge],
        (aux, near0, far0, *pieces), hbm, hbm, scratch, 3 + 3 * n,
    )
    near, far = beside(near, far)
    outs = call(
        functools.partial(sweep_kernel, geo, False, tiles, points, table), "sweep_closing",
        [(4, 2, planes * geo.back, LANES)] * n, (aux, near0, far0, own, near, far), hbm, hbm, scratch, 3 + 3 * n,
    )
    outs = [across(k, outs[k]) if k else outs[k] for k in range(n)]
    (result,) = call(
        functools.partial(unpack_kernel, geo), "unpack", [(1, 4, planes, depth, width)], outs, hbm, vmem,
        [(n, 4, 2, planes * geo.back, LANES)], n,
    )
    return result


def solution(mesh):
    in_specs = (
        P(None, "space", None, None),
        P("node", None, "space", None, None),
        P("space", None, None),
        P("space", None, None),
    )
    out_specs = P("node", None, "space", None, None)
    return jax.shard_map(
        on_device, mesh=mesh, in_specs=in_specs, out_specs=out_specs, check_vma=False
    )
```

```python
import functools
import math

import jax
import jax.numpy as jnp
import numpy as np
from jax import lax
from jax.experimental import pallas as pl
from jax.experimental.pallas import tpu as pltpu
from jax.sharding import PartitionSpec as P

SWEEPS = 2
JACOBI = 3
LANES = 128
VMEM_SLACK = 2 << 20

advect_rate = 0.25
buoyancy = 0.5
heating = 1.0
diffusion = (0.5, 0.5, 0.5, 0.35)


def legendre_value(order, place):
    previous = 1.0
    current = place
    for degree in range(1, order):
        following = ((2 * degree + 1) * place * current - degree * previous) / (degree + 1)
        previous = current
        current = following
    return current


def radau_tables(count):

    def radau_poly(place):
        return legendre_value(count, place) - legendre_value(count - 1, place)

    samples = 4000 * count
    roots_found = []
    left_end = -1.0
    left_value = radau_poly(left_end)
    for index in range(1, samples + 1):
        right_end = -1.0 + (2.0 - 1e-07) * index / samples
        right_value = radau_poly(right_end)
        if left_value * right_value < 0.0:
            low_end = left_end
            high_end = right_end
            low_value = left_value
            for repeat in range(200):
                middle = 0.5 * (low_end + high_end)
                middle_value = radau_poly(middle)
                if low_value * middle_value <= 0.0:
                    high_end = middle
                else:
                    low_end = middle
                    low_value = middle_value
            roots_found.append(0.5 * (low_end + high_end))
        left_end = right_end
        left_value = right_value
    points = [(value + 1.0) / 2.0 for value in roots_found[: count - 1]] + [1.0]
    table = []
    for row in range(count):
        table.append([0.0] * count)
    for column in range(count):
        coefficients = [1.0]
        for other in range(count):
            if other == column:
                continue
            scale = 1.0 / (points[column] - points[other])
            widened = [0.0] * (len(coefficients) + 1)
            for index in range(len(coefficients)):
                widened[index + 1] += coefficients[index] * scale
                widened[index] -= points[other] * coefficients[index] * scale
            coefficients = widened
        for row in range(count):
            total = 0.0
            for index in range(len(coefficients)):
                total += coefficients[index] * points[row] ** (index + 1) / (index + 1)
            table[row][column] = total
    return (points, table)


def size_of(shape):
    return math.prod(getattr(shape, "shape", shape))


def round_up(value, step):
    return -(-value // step) * step


class Geometry:
    def __init__(self, nodes, planes, depth):
        overlap = SWEEPS * JACOBI if nodes > 1 else 0
        self.nodes, self.planes, self.depth = nodes, planes, depth
        self.window = -(-(depth + 2 * overlap * (nodes - 1)) // nodes)
        step = self.window - 2 * overlap
        assert step > 0 and planes >= JACOBI
        self.offset = [min(p * step, depth - self.window) for p in range(nodes)]
        first = [0] + [p * step + overlap for p in range(1, nodes)]
        last = first[1:] + [depth]
        self.first, self.count = first, [b - a for a, b in zip(first, last)]
        self.stride = self.window + 1
        while (planes * self.stride) % 8:
            self.stride += 1
        self.rows = planes * self.stride
        self.side = round_up(JACOBI * self.stride, 8)
        self.low = 8 + self.side
        self.total = self.low + self.rows + self.side + 8
        self.back = max(self.count)
        while (planes * self.back) % 8:
            self.back += 1

    def trims(self, closing, reach):
        packed, cuts = 0, []
        for d in range(1, reach + 1):
            cut = closing * JACOBI + d
            cuts.append((d, cut, packed, self.window - cut))
            packed += self.window - cut
        return cuts, round_up(packed, 8)

    def mixed(self):
        row, parts = 0, []
        for f in range(10):
            cuts, count = self.trims(False, JACOBI if f < 4 else JACOBI - 1)
            for h in range(2):
                parts.append((f, h, cuts, row))
                row += count
        self.mixed_rows = row
        return parts

    def span(self, reach):
        begin = (self.low - reach * self.stride) // 8 * 8
        end = round_up(self.low + (self.planes + reach) * self.stride, 8)
        assert begin - self.stride >= 0 and end + self.stride <= self.total
        return begin, end

    def early(self, upper):
        begin, end = self.span(JACOBI - 1)
        second_begin, second_end = self.span(JACOBI - 2)
        if upper:
            end = (self.low + (self.planes - 1) * self.stride) // 8 * 8
            second_end = (end - self.stride) // 8 * 8
        else:
            begin = round_up(self.low + self.stride, 8)
            second_begin = round_up(begin + self.stride, 8)
        return (begin, end), (second_begin, second_end)

    def late(self, upper):
        rest = []
        for whole, part in zip((self.span(JACOBI - 1), self.span(JACOBI - 2)), self.early(upper)):
            rest.append((part[1], whole[1]) if upper else (whole[0], part[0]))
        return rest


def copy_all(pairs, sems):
    copies = [pltpu.make_async_copy(source, target, sems.at[i]) for i, (source, target) in enumerate(pairs)]
    for copy in copies:
        copy.start()
    for copy in copies:
        copy.wait()


def pack_kernel(geo, guess_ref, *refs):
    *outs, windows, sems = refs
    me = lax.axis_index("node")
    blank = jnp.zeros((geo.stride - geo.window, LANES), jnp.float32)
    for p in range(geo.nodes):
        for f in range(4):
            for x in range(geo.planes):
                for h in range(2):
                    at = x * geo.stride
                    windows[p, f, h, at : at + geo.window] = guess_ref[
                        0, f, x, geo.offset[p] : geo.offset[p] + geo.window, h * LANES : (h + 1) * LANES
                    ]
                    windows[p, f, h, at + geo.window : at + geo.stride] = blank
    copy_all([(windows.at[me ^ k], outs[k - 1]) for k in range(1, geo.nodes)], sems)


def send_rows(geo, odd):
    far = geo.rows - geo.side
    return pl.multiple_of(far * (1 - odd), 8), pl.multiple_of(far * odd, 8)


def each_place(me, odd, body):
    for upper in (False, True):
        for lowest in (False, True):
            pl.when((odd == int(upper)) & ((me == 0) == lowest))(functools.partial(body, upper, lowest))


def trim(geo, cuts, upper, lowest, source, at, target, to=0):
    for d, cut, packed, count in cuts:
        plane = geo.planes - d if upper else d - 1
        row = at + plane * geo.stride + (0 if lowest else cut)
        target[to + packed : to + packed + count] = source[row : row + count]


def place(geo, cuts, upper, lowest, source, target, start=0):
    for d, cut, packed, count in cuts:
        plane = geo.planes - 1 + d if upper else -d
        row = geo.low + plane * geo.stride + (0 if lowest else cut)
        target[row : row + count] = source[start + packed : start + packed + count]


def trim_kernel(geo, own_ref, far_ref):
    def body(upper, lowest):
        for f in range(4):
            for h in range(2):
                trim(geo, geo.trims(False, JACOBI)[0], upper, lowest, own_ref.at[f, h], 0, far_ref.at[f, h])

    each_place(lax.axis_index("node"), lax.axis_index("space") % 2, body)


def halo_rows(geo, odd):
    below, above = geo.low - geo.side, geo.low + geo.rows
    return (
        pl.multiple_of(above + (below - above) * odd, 8),
        pl.multiple_of(below + (above - below) * odd, 8),
    )


def pack_own_kernel(
    geo, guess_hbm, start_hbm, heat_hbm, solid_hbm, own_ref, aux_ref, near_ref, far_ref,
    guess_ref, start_ref, heat_ref, solid_ref, packed, sems,
):
    me, odd = lax.axis_index("node"), lax.axis_index("space") % 2
    copy_all(
        [(guess_hbm, guess_ref), (start_hbm, start_ref), (heat_hbm, heat_ref), (solid_hbm, solid_ref)], sems
    )
    blank = jnp.zeros((geo.stride - geo.window, LANES), jnp.float32)
    for p in range(geo.nodes):

        @pl.when(me == p)
        def _():
            rows = slice(geo.offset[p], geo.offset[p] + geo.window)
            for x in range(geo.planes):
                for h in range(2):
                    at = x * geo.stride
                    lanes = slice(h * LANES, (h + 1) * LANES)
                    for f in range(4):
                        packed[f, h, at : at + geo.window] = guess_ref[0, f, x, rows, lanes]
                        packed[4 + f, h, at : at + geo.window] = start_ref[f, x, rows, lanes]
                    packed[8, h, at : at + geo.window] = heating * heat_ref[x, rows, lanes].astype(jnp.float32)
                    packed[9, h, at : at + geo.window] = 1.0 - solid_ref[x, rows, lanes].astype(jnp.float32)
                    for f in range(10):
                        packed[f, h, at + geo.window : at + geo.stride] = blank

    near, far = send_rows(geo, odd)
    copies = [
        pltpu.make_async_copy(packed.at[:, :, pl.ds(near, geo.side)], near_ref, sems.at[0]),
        pltpu.make_async_copy(packed.at[pl.ds(0, 4)], own_ref, sems.at[1]),
        pltpu.make_async_copy(packed.at[pl.ds(4, 6)], aux_ref, sems.at[2]),
    ]
    for copy in copies:
        copy.start()

    def body(upper, lowest):
        for f, h, cuts, row in geo.mixed():
            trim(geo, cuts, upper, lowest, packed.at[f, h], 0, far_ref, row)

    each_place(me, odd, body)
    for copy in copies:
        copy.wait()


def pick(index, values):
    chosen = jnp.float32(values[-1])
    for i in reversed(range(len(values) - 1)):
        chosen = jnp.where(index == i, jnp.float32(values[i]), chosen)
    return chosen


def lane_sides(a, b):
    lane = lax.broadcasted_iota(jnp.int32, (8, LANES), 1)
    is_first, is_last = lane == 0, lane == LANES - 1
    ra, rb = pltpu.roll(a, 1, 1), pltpu.roll(b, 1, 1)
    la, lb = pltpu.roll(a, LANES - 1, 1), pltpu.roll(b, LANES - 1, 1)
    minus = (jnp.where(is_first, 0.0, ra), jnp.where(is_first, ra, rb))
    plus = (jnp.where(is_last, lb, la), jnp.where(is_last, 0.0, lb))
    return minus, plus


class Steps:
    def __init__(self, geo, points, table, aux, mask, field, tend, base, first):
        self.geo, self.points, self.table = geo, points, table
        self.aux, self.mask, self.field, self.tend, self.base, self.first = aux, mask, field, tend, base, first

    def slopes(self, j, begin, end):
        field, aux, stride = self.field, self.aux, self.geo.stride
        for r in range(begin, end, 8):
            rows = pl.ds(r, 8)
            vel = []
            for h in range(2):
                vel.append([(-0.5 * advect_rate) * field[j, f, h, rows] for f in range(3)])
            for f in range(4):
                centre = [field[j, f, h, rows] for h in range(2)]
                minus, plus = lane_sides(centre[0], centre[1])
                for h in range(2):
                    xp, xm = field[j, f, h, pl.ds(r + stride, 8)], field[j, f, h, pl.ds(r - stride, 8)]
                    zp, zm = field[j, f, h, pl.ds(r + 1, 8)], field[j, f, h, pl.ds(r - 1, 8)]
                    near = (xp + xm) + (zp + zm) + (plus[h] + minus[h])
                    moved = vel[h][0] * (xp - xm) + vel[h][1] * (plus[h] - minus[h]) + vel[h][2] * (zp - zm)
                    total = moved + diffusion[f] * (near - 6.0 * centre[h])
                    if f == 2:
                        total = total + buoyancy * field[j, 3, h, rows]
                    if f == 3:
                        total = total + aux[4, h, rows]
                    else:
                        total = total * aux[5, h, rows]
                    self.tend[j, f, h, rows] = total
                    self.base[j, f, h, rows] = near

    def quadrature(self, begin, end):
        n, points, table = self.geo.nodes, self.points, self.table

        def body(t, _):
            rows = pl.ds(pl.multiple_of(t * 8, 8), 8)
            inside = self.mask[rows]
            for f in range(4):
                scale = [inside * (1.0 / (1.0 + 6.0 * points[m] * diffusion[f])) for m in range(n)]
                for h in range(2):
                    slopes = [self.tend[j, f, h, rows] for j in range(n)]
                    begun = self.aux[f, h, rows]
                    for m in range(n):
                        c = points[m] * diffusion[f]
                        total = begun + (6.0 * c) * self.field[m, f, h, rows]
                        for j in range(n):
                            total = total + table[m][j] * slopes[j]
                        total = total * scale[m]
                        self.first[m, f, h, rows] = total
                        self.base[m, f, h, rows] = total - (c * scale[m]) * self.base[m, f, h, rows]
            return 0

        lax.fori_loop(begin // 8, end // 8, body, 0)

    def weights(self, m):
        return [pick(m, [p * d / (1.0 + 6.0 * p * d) for p in self.points]) for d in diffusion]

    def relax_rows(self, source, target, m, f, r, weight, to):
        stride = self.geo.stride
        minus, plus = lane_sides(source[m, f, 0, pl.ds(r, 8)], source[m, f, 1, pl.ds(r, 8)])
        for h in range(2):
            near = (
                (source[m, f, h, pl.ds(r + stride, 8)] + source[m, f, h, pl.ds(r - stride, 8)])
                + (source[m, f, h, pl.ds(r + 1, 8)] + source[m, f, h, pl.ds(r - 1, 8)])
                + (plus[h] + minus[h])
            )
            target[m, f, h, pl.ds(to, 8)] = self.base[m, f, h, pl.ds(r, 8)] + weight * near

    def relax(self, source, target, m, begin, end):
        weight = self.weights(m)
        for r in range(begin, end, 8):
            inside = self.mask[pl.ds(r, 8)]
            for f in range(4):
                self.relax_rows(source, target, m, f, r, inside * weight[f], r)


def each_node(count, body):
    def step(i, _):
        body(i)
        return 0

    lax.fori_loop(0, count, step, 0)


def by_side(odd, body):
    for upper in (False, True):
        pl.when(odd == int(upper))(functools.partial(body, upper))


def start_kernel(geo, opening, tiles, points, table, *refs):
    n, low, side = geo.nodes, geo.low, geo.side
    me, tile = lax.axis_index("node"), lax.axis_index("space")
    odd = tile % 2
    near, far = halo_rows(geo, odd)
    near_from, _ = send_rows(geo, 1 - odd)
    own_rows, near_rows, far_rows = pl.ds(low, geo.rows), pl.ds(near, side), pl.ds(far, side)
    pairs = []
    if opening:
        aux_ref, near0_ref, far0_ref, own0_ref, *rest, aux, mask, field, tend, base, first, sems = refs
        pairs = [(aux_ref, aux.at[:, :, own_rows]), (near0_ref.at[pl.ds(4, 6)], aux.at[:, :, near_rows])]
        fars = []
        for k in range(n):
            sources = own0_ref, near0_ref.at[pl.ds(0, 4)]
            if k:
                own_ref, near_ref, *rest = rest
                sources = own_ref, near_ref.at[:, :, pl.ds(near_from, side)]
            if 0 < k < n - 1:
                far_ref, *rest = rest
                fars.append(far_ref)
            pairs += zip(sources, [field.at[me ^ k, :, :, rows] for rows in (own_rows, near_rows)])
    else:
        aux, mask, own_ref, near_ref, field, tend, base, first, sems = refs
        for k in range(n):
            pairs += [(own_ref.at[k], field.at[k, :, :, own_rows]), (near_ref.at[k], field.at[k, :, :, near_rows])]
    copies = [pltpu.make_async_copy(source, target, sems.at[i]) for i, (source, target) in enumerate(pairs)]
    for copy in copies:
        copy.start()

    field[:, :, :, far_rows] = jnp.zeros((n, 4, 2, side, LANES), jnp.float32)
    if opening:
        aux[:, :, far_rows] = jnp.zeros((6, 2, side, LANES), jnp.float32)
        mask[...] = jnp.zeros(mask.shape, jnp.float32)
        for q in range(-JACOBI, geo.planes + JACOBI):
            there = jnp.float32(1.0)
            if q < 0:
                there = jnp.where(tile > 0, 1.0, 0.0)
            if q >= geo.planes:
                there = jnp.where(tile < tiles - 1, 1.0, 0.0)
            at = low + q * geo.stride
            mask[at : at + geo.window] = jnp.full((geo.window, LANES), there, jnp.float32)

        def unpack_far(upper, lowest):
            for f, h, cuts, row in geo.mixed():
                place(geo, cuts, upper, lowest, far0_ref, aux.at[f - 4, h] if f >= 4 else field.at[me, f, h], row)
            for k in range(1, n - 1):
                for f in range(4):
                    for h in range(2):
                        cuts = geo.trims(False, JACOBI)[0]
                        place(geo, cuts, upper, lowest, fars[k - 1].at[f, h], field.at[me ^ k, f, h])

        each_place(me, odd, unpack_far)
        for copy in copies[:2]:
            copy.wait()

    steps = Steps(geo, points, table, aux, mask, field, tend, base, first)
    shift = 2 if opening else 0

    def arrive(k, j):
        for i, rows in enumerate((own_rows, near_rows)):
            part = field.at[j, :, :, rows]
            pltpu.make_async_copy(part, part, sems.at[shift + 2 * k + i]).wait()

    if opening:

        def whole(k):
            arrive(k, me ^ k)
            steps.slopes(me ^ k, *geo.span(JACOBI - 1))

        each_node(n - 1, whole)
        arrive(n - 1, me ^ (n - 1))

    def early(upper):
        rows, second = geo.early(upper)
        if opening:
            steps.slopes(me ^ (n - 1), *rows)
        else:

            def part(k):
                arrive(k, k)
                steps.slopes(k, *rows)

            each_node(n, part)
        steps.quadrature(*rows)
        each_node(n, lambda m: steps.relax(first, tend, m, *second))

    by_side(odd, early)


def finish_kernel(geo, opening, points, table, aux, mask, *refs):
    n, stride, low, side = geo.nodes, geo.stride, geo.low, geo.side
    me, odd = lax.axis_index("node"), lax.axis_index("space") % 2
    far_ref = refs[4]
    field, tend, base, first, *outs, sems = refs[5:]
    steps = Steps(geo, points, table, aux, mask, field, tend, base, first)

    def unpack_far(upper, lowest):
        cuts = geo.trims(not opening, JACOBI)[0]
        for f in range(4):
            for h in range(2):
                if opening:
                    place(geo, cuts, upper, lowest, far_ref.at[f, h], field.at[me ^ (n - 1), f, h])
                else:
                    for k in range(n):
                        place(geo, cuts, upper, lowest, far_ref.at[k, f, h], field.at[k, f, h])

    each_place(me, odd, unpack_far)

    def late(upper):
        rows, second = geo.late(upper)
        if opening:
            steps.slopes(me ^ (n - 1), *rows)
        else:
            each_node(n, lambda j: steps.slopes(j, *rows))
        steps.quadrature(*rows)
        each_node(n, lambda m: steps.relax(first, tend, m, *second))

    by_side(odd, late)

    if opening:
        out_ref, near_out, far_out = outs
        near_row = send_rows(geo, odd)[0]

        def results(m):
            copies = []
            for i, (row, count, ref) in enumerate(((near_row, side, near_out), (0, geo.rows, out_ref))):
                part = first.at[m, :, :, pl.ds(pl.multiple_of(low + row, 8), count)]
                copies.append(pltpu.make_async_copy(part, ref.at[m], sems.at[2 * m + i]))
            return copies

        def third(m):
            steps.relax(tend, first, m, *geo.span(0))
            for copy in results(m):
                copy.start()

            def pack_far(upper, lowest):
                for f in range(4):
                    for h in range(2):
                        cuts = geo.trims(True, JACOBI)[0]
                        trim(geo, cuts, upper, lowest, first.at[m, f, h], low, far_out.at[m, f, h])

            each_place(me, odd, pack_far)

        each_node(n, third)
        for m in range(n):
            for copy in results(m):
                copy.wait()
        return

    done = pl.ds(0, geo.planes * geo.back)
    for start in sorted({a - b for a, b in zip(geo.first, geo.offset)}):
        hit = [p for p in range(n) if geo.first[p] - geo.offset[p] == start]
        chosen = functools.reduce(jnp.logical_or, [me == p for p in hit])

        @pl.when(chosen)
        def _():
            def third(i):
                k = n - 1 - i
                m = me ^ k
                weight = steps.weights(m)
                for x in range(geo.planes):
                    for o in [*range(0, geo.back - 8, 8), geo.back - 8]:
                        for f in range(4):
                            r = low + x * stride + start + o
                            steps.relax_rows(tend, first, m, f, r, weight[f], x * geo.back + o)
                for other in range(n):

                    @pl.when(k == other)
                    def _():
                        pltpu.make_async_copy(first.at[m, :, :, done], outs[other], sems.at[other]).start()

            each_node(n, third)

    for k in range(n):
        pltpu.make_async_copy(first.at[me ^ k, :, :, done], outs[k], sems.at[k]).wait()


def unpack_kernel(geo, *refs):
    ins, (out_ref, pieces, sems) = refs[: geo.nodes], refs[geo.nodes :]
    me = lax.axis_index("node")
    copy_all([(ins[k], pieces.at[me ^ k]) for k in range(geo.nodes)], sems)
    for p in range(geo.nodes):
        for f in range(4):
            for x in range(geo.planes):
                for h in range(2):
                    at = x * geo.back
                    out_ref[0, f, x, geo.first[p] : geo.first[p] + geo.count[p], h * LANES : (h + 1) * LANES] = pieces[
                        p, f, h, at : at + geo.count[p]
                    ]


def on_device(start, guess, heat_mask, solid_mask):
    n = lax.axis_size("node")
    tiles = lax.axis_size("space")
    planes, depth, width = guess.shape[2:]
    assert width == 2 * LANES and tiles % 2 == 0 and n & (n - 1) == 0
    geo = Geometry(n, planes, depth)
    points_list, table_list = radau_tables(n)
    table = [[float(np.float32(v)) for v in row] for row in table_list]
    points = [float(np.float32(v)) for v in points_list]
    f32 = jnp.float32
    vmem, free = pl.BlockSpec(memory_space=pltpu.VMEM), pl.BlockSpec(memory_space=pl.ANY)

    def call(kernel, name, outs, out_specs, ins, in_specs, scratch, copies, aliases={}):
        held = list(scratch)
        semaphores = [pltpu.SemaphoreType.DMA((copies,))] if copies else []
        return pl.pallas_call(
            kernel, name=name,
            out_shape=[jax.ShapeDtypeStruct(shape, f32) for shape in outs], in_specs=in_specs, out_specs=out_specs,
            input_output_aliases=aliases,
            scratch_shapes=[a if hasattr(a, "memory_space") else pltpu.VMEM(a, f32) for a in scratch] + semaphores,
            compiler_params=pltpu.CompilerParams(vmem_limit_bytes=VMEM_SLACK + 4 * sum(map(size_of, held))),
        )(*ins)

    def across(k, value):
        return lax.ppermute(value, "node", [(i, i ^ k) for i in range(n)])

    chip = [(i, i ^ 1) for i in range(tiles)]
    links = [(i, i + 1) for i in range(1, tiles - 1, 2)] + [(i + 1, i) for i in range(1, tiles - 1, 2)]

    def beside(near, far):
        return lax.ppermute(near, "space", chip), lax.ppermute(far, "space", links)

    piece = (4, 2, geo.rows, LANES)
    sends = call(
        functools.partial(pack_kernel, geo), "pack", [piece] * (n - 1), [free] * (n - 1), (guess,), [vmem],
        [(n,) + piece], n - 1,
    )
    geo.mixed()
    masks = pltpu.VMEM(heat_mask.shape, jnp.int32)
    own, aux, near, far = call(
        functools.partial(pack_own_kernel, geo), "pack_own",
        [piece, (6,) + piece[1:], (10, 2, geo.side, LANES), (geo.mixed_rows, LANES)], [free, free, free, vmem],
        (guess, start, heat_mask, solid_mask), [pl.BlockSpec(memory_space=pltpu.HBM)] * 4,
        [guess.shape, start.shape, masks, masks, (10,) + piece[1:]], 4,
    )
    near0, far0 = beside(near, far)

    owns = {0: own}
    wave = []
    for hops in range(1, n.bit_length()):
        group = [k for k in range(1, n) if k.bit_count() == hops]
        gated = lax.optimization_barrier([sends[k - 1] for k in group] + wave)
        wave = [across(k, value) for k, value in zip(group, gated)]
        owns.update(zip(group, wave))
    pieces, specs = [own], [free]
    for k in range(1, n):
        (far,) = call(
            functools.partial(trim_kernel, geo), "trim", [(4, 2, geo.trims(False, JACOBI)[1], LANES)], [vmem],
            (owns[k],), [vmem], [], 0,
        )
        held, far = lax.optimization_barrier((owns[k], far))
        near, far = beside(held, far)
        pieces += [owns[k], near]
        specs += [free, free]
        if k < n - 1:
            pieces.append(far)
            specs.append(vmem)

    big = (n, 4, 2, geo.total, LANES)
    state, kept = [big] * 4, [(6, 2, geo.total, LANES), (geo.total, LANES)]
    sent = (n, 4, 2, geo.trims(True, JACOBI)[1], LANES)
    aux, mask, *held = call(
        functools.partial(start_kernel, geo, True, tiles, points, table), "opening_start", kept + state, [vmem] * 6,
        (aux, near0, far0, *pieces), [free, free, vmem, *specs], [], 2 + 2 * n,
    )
    aliases = {2 + i: i for i in range(4)}
    own, near, far = call(
        functools.partial(finish_kernel, geo, True, points, table), "opening_finish",
        state + [(n,) + piece, (n, 4, 2, geo.side, LANES), sent], [vmem] * 4 + [free, free, vmem],
        (aux, mask, *held, far), [vmem] * 7, [], 2 * n, aliases,
    )[4:]
    near, far = beside(near, far)
    held = call(
        functools.partial(start_kernel, geo, False, tiles, points, table), "closing_start", state, [vmem] * 4,
        (aux, mask, own, near), [vmem, vmem, free, free], [], 2 * n,
    )
    outs = call(
        functools.partial(finish_kernel, geo, False, points, table), "closing_finish",
        state + [(4, 2, planes * geo.back, LANES)] * n, [vmem] * 4 + [free] * n,
        (aux, mask, *held, far), [vmem] * 7, [], n, aliases,
    )[4:]
    outs = [across(k, outs[k]) if k else outs[k] for k in range(n)]
    (result,) = call(
        functools.partial(unpack_kernel, geo), "unpack", [(1, 4, planes, depth, width)], [vmem], outs, [free] * n,
        [(n, 4, 2, planes * geo.back, LANES)], n,
    )
    return result


def solution(mesh):
    in_specs = (
        P(None, "space", None, None),
        P("node", None, "space", None, None),
        P("space", None, None),
        P("space", None, None),
    )
    out_specs = P("node", None, "space", None, None)
    return jax.shard_map(
        on_device, mesh=mesh, in_specs=in_specs, out_specs=out_specs, check_vma=False
    )
```

```python
import functools
import math

import jax
import jax.numpy as jnp
import numpy as np
from jax import lax
from jax.experimental import pallas as pl
from jax.experimental.pallas import tpu as pltpu
from jax.sharding import PartitionSpec as P

SWEEPS = 2
JACOBI = 3
LANES = 128
VMEM_SLACK = 2 << 20

advect_rate = 0.25
buoyancy = 0.5
heating = 1.0
diffusion = (0.5, 0.5, 0.5, 0.35)


def legendre_value(order, place):
    previous = 1.0
    current = place
    for degree in range(1, order):
        following = ((2 * degree + 1) * place * current - degree * previous) / (degree + 1)
        previous = current
        current = following
    return current


def radau_tables(count):

    def radau_poly(place):
        return legendre_value(count, place) - legendre_value(count - 1, place)

    samples = 4000 * count
    roots_found = []
    left_end = -1.0
    left_value = radau_poly(left_end)
    for index in range(1, samples + 1):
        right_end = -1.0 + (2.0 - 1e-07) * index / samples
        right_value = radau_poly(right_end)
        if left_value * right_value < 0.0:
            low_end = left_end
            high_end = right_end
            low_value = left_value
            for repeat in range(200):
                middle = 0.5 * (low_end + high_end)
                middle_value = radau_poly(middle)
                if low_value * middle_value <= 0.0:
                    high_end = middle
                else:
                    low_end = middle
                    low_value = middle_value
            roots_found.append(0.5 * (low_end + high_end))
        left_end = right_end
        left_value = right_value
    points = [(value + 1.0) / 2.0 for value in roots_found[: count - 1]] + [1.0]
    table = []
    for row in range(count):
        table.append([0.0] * count)
    for column in range(count):
        coefficients = [1.0]
        for other in range(count):
            if other == column:
                continue
            scale = 1.0 / (points[column] - points[other])
            widened = [0.0] * (len(coefficients) + 1)
            for index in range(len(coefficients)):
                widened[index + 1] += coefficients[index] * scale
                widened[index] -= points[other] * coefficients[index] * scale
            coefficients = widened
        for row in range(count):
            total = 0.0
            for index in range(len(coefficients)):
                total += coefficients[index] * points[row] ** (index + 1) / (index + 1)
            table[row][column] = total
    return (points, table)


def size_of(shape):
    return math.prod(getattr(shape, "shape", shape))


def round_up(value, step):
    return -(-value // step) * step


class Geometry:
    def __init__(self, nodes, planes, depth):
        overlap = SWEEPS * JACOBI if nodes > 1 else 0
        self.nodes, self.planes, self.depth = nodes, planes, depth
        self.window = -(-(depth + 2 * overlap * (nodes - 1)) // nodes)
        step = self.window - 2 * overlap
        assert step > 0 and planes >= JACOBI
        self.offset = [min(p * step, depth - self.window) for p in range(nodes)]
        first = [0] + [p * step + overlap for p in range(1, nodes)]
        last = first[1:] + [depth]
        self.first, self.count = first, [b - a for a, b in zip(first, last)]
        self.stride = self.window + 1
        while (planes * self.stride) % 8:
            self.stride += 1
        self.rows = planes * self.stride
        self.side = round_up(JACOBI * self.stride, 8)
        self.low = 8 + self.side
        self.total = self.low + self.rows + self.side + 8
        self.back = max(self.count)
        while (planes * self.back) % 8:
            self.back += 1

    def trims(self, closing, reach):
        packed, cuts = 0, []
        for d in range(1, reach + 1):
            cut = closing * JACOBI + d
            cuts.append((d, cut, packed, self.window - cut))
            packed += self.window - cut
        return cuts, packed

    def mixed(self):
        row, parts = 0, []
        for f in range(10):
            cuts, count = self.trims(False, JACOBI if f < 4 else JACOBI - 1)
            for h in range(2):
                parts.append((f, h, cuts, row))
                row += count
        self.mixed_rows = round_up(row, 8)
        return parts

    def fields(self, closing):
        cuts, count = self.trims(closing, JACOBI)
        return [(f, h, cuts, (2 * f + h) * count) for f in range(4) for h in range(2)], round_up(8 * count, 8)

    def span(self, reach):
        begin = (self.low - reach * self.stride) // 8 * 8
        end = round_up(self.low + (self.planes + reach) * self.stride, 8)
        assert begin - self.stride >= 0 and end + self.stride <= self.total
        return begin, end

    def early(self, upper):
        begin, end = self.span(JACOBI - 1)
        second_begin, second_end = self.span(JACOBI - 2)
        if upper:
            end = (self.low + (self.planes - 1) * self.stride) // 8 * 8
            second_end = (end - self.stride) // 8 * 8
        else:
            begin = round_up(self.low + self.stride, 8)
            second_begin = round_up(begin + self.stride, 8)
        return (begin, end), (second_begin, second_end)

    def late(self, upper):
        rest = []
        for whole, part in zip((self.span(JACOBI - 1), self.span(JACOBI - 2)), self.early(upper)):
            rest.append((part[1], whole[1]) if upper else (whole[0], part[0]))
        return rest


def copy_all(pairs, sems):
    copies = [pltpu.make_async_copy(source, target, sems.at[i]) for i, (source, target) in enumerate(pairs)]
    for copy in copies:
        copy.start()
    for copy in copies:
        copy.wait()


def pack_kernel(geo, guess_ref, *refs):
    *outs, windows, sems = refs
    me = lax.axis_index("node")
    blank = jnp.zeros((geo.stride - geo.window, LANES), jnp.float32)
    for p in range(geo.nodes):
        for f in range(4):
            for x in range(geo.planes):
                for h in range(2):
                    at = x * geo.stride
                    windows[p, f, h, at : at + geo.window] = guess_ref[
                        0, f, x, geo.offset[p] : geo.offset[p] + geo.window, h * LANES : (h + 1) * LANES
                    ]
                    windows[p, f, h, at + geo.window : at + geo.stride] = blank
    copy_all([(windows.at[me ^ k], outs[k - 1]) for k in range(1, geo.nodes)], sems)


def send_rows(geo, odd):
    far = geo.rows - geo.side
    return pl.multiple_of(far * (1 - odd), 8), pl.multiple_of(far * odd, 8)


def each_place(me, odd, body):
    for upper in (False, True):
        for lowest in (False, True):
            pl.when((odd == int(upper)) & ((me == 0) == lowest))(functools.partial(body, upper, lowest))


def trim(geo, cuts, upper, lowest, source, at, target, to=0):
    for d, cut, packed, count in cuts:
        plane = geo.planes - d if upper else d - 1
        row = at + plane * geo.stride + (0 if lowest else cut)
        target[to + packed : to + packed + count] = source[row : row + count]


def place(geo, cuts, upper, lowest, source, target, start=0):
    for d, cut, packed, count in cuts:
        plane = geo.planes - 1 + d if upper else -d
        row = geo.low + plane * geo.stride + (0 if lowest else cut)
        target[row : row + count] = source[start + packed : start + packed + count]


def trim_kernel(geo, own_ref, far_ref):
    def body(upper, lowest):
        for f, h, cuts, row in geo.fields(False)[0]:
            trim(geo, cuts, upper, lowest, own_ref.at[f, h], 0, far_ref, row)

    each_place(lax.axis_index("node"), lax.axis_index("space") % 2, body)


def halo_rows(geo, odd):
    below, above = geo.low - geo.side, geo.low + geo.rows
    return (
        pl.multiple_of(above + (below - above) * odd, 8),
        pl.multiple_of(below + (above - below) * odd, 8),
    )


def pack_own_kernel(
    geo, guess_hbm, start_hbm, heat_hbm, solid_hbm, own_ref, aux_ref, near_ref, far_ref,
    guess_ref, start_ref, heat_ref, solid_ref, packed, sems,
):
    me, odd = lax.axis_index("node"), lax.axis_index("space") % 2
    copy_all(
        [(guess_hbm, guess_ref), (start_hbm, start_ref), (heat_hbm, heat_ref), (solid_hbm, solid_ref)], sems
    )
    blank = jnp.zeros((geo.stride - geo.window, LANES), jnp.float32)
    for p in range(geo.nodes):

        @pl.when(me == p)
        def _():
            rows = slice(geo.offset[p], geo.offset[p] + geo.window)
            for x in range(geo.planes):
                for h in range(2):
                    at = x * geo.stride
                    lanes = slice(h * LANES, (h + 1) * LANES)
                    for f in range(4):
                        packed[f, h, at : at + geo.window] = guess_ref[0, f, x, rows, lanes]
                        packed[4 + f, h, at : at + geo.window] = start_ref[f, x, rows, lanes]
                    packed[8, h, at : at + geo.window] = heating * heat_ref[x, rows, lanes].astype(jnp.float32)
                    packed[9, h, at : at + geo.window] = 1.0 - solid_ref[x, rows, lanes].astype(jnp.float32)
                    for f in range(10):
                        packed[f, h, at + geo.window : at + geo.stride] = blank

    near, far = send_rows(geo, odd)
    copies = [
        pltpu.make_async_copy(packed.at[:, :, pl.ds(near, geo.side)], near_ref, sems.at[0]),
        pltpu.make_async_copy(packed.at[pl.ds(0, 4)], own_ref, sems.at[1]),
        pltpu.make_async_copy(packed.at[pl.ds(4, 6)], aux_ref, sems.at[2]),
    ]
    for copy in copies:
        copy.start()

    def body(upper, lowest):
        for f, h, cuts, row in geo.mixed():
            trim(geo, cuts, upper, lowest, packed.at[f, h], 0, far_ref, row)

    each_place(me, odd, body)
    for copy in copies:
        copy.wait()


def pick(index, values):
    chosen = jnp.float32(values[-1])
    for i in reversed(range(len(values) - 1)):
        chosen = jnp.where(index == i, jnp.float32(values[i]), chosen)
    return chosen


def lane_sides(a, b):
    lane = lax.broadcasted_iota(jnp.int32, (8, LANES), 1)
    is_first, is_last = lane == 0, lane == LANES - 1
    ra, rb = pltpu.roll(a, 1, 1), pltpu.roll(b, 1, 1)
    la, lb = pltpu.roll(a, LANES - 1, 1), pltpu.roll(b, LANES - 1, 1)
    minus = (jnp.where(is_first, 0.0, ra), jnp.where(is_first, ra, rb))
    plus = (jnp.where(is_last, lb, la), jnp.where(is_last, 0.0, lb))
    return minus, plus


class Steps:
    def __init__(self, geo, points, table, aux, mask, field, tend, base, first):
        self.geo, self.points, self.table = geo, points, table
        self.aux, self.mask, self.field, self.tend, self.base, self.first = aux, mask, field, tend, base, first

    def slopes(self, j, begin, end):
        field, aux, stride = self.field, self.aux, self.geo.stride
        for r in range(begin, end, 8):
            rows = pl.ds(r, 8)
            vel = []
            for h in range(2):
                vel.append([(-0.5 * advect_rate) * field[j, f, h, rows] for f in range(3)])
            for f in range(4):
                centre = [field[j, f, h, rows] for h in range(2)]
                minus, plus = lane_sides(centre[0], centre[1])
                for h in range(2):
                    xp, xm = field[j, f, h, pl.ds(r + stride, 8)], field[j, f, h, pl.ds(r - stride, 8)]
                    zp, zm = field[j, f, h, pl.ds(r + 1, 8)], field[j, f, h, pl.ds(r - 1, 8)]
                    near = (xp + xm) + (zp + zm) + (plus[h] + minus[h])
                    moved = vel[h][0] * (xp - xm) + vel[h][1] * (plus[h] - minus[h]) + vel[h][2] * (zp - zm)
                    total = moved + diffusion[f] * (near - 6.0 * centre[h])
                    if f == 2:
                        total = total + buoyancy * field[j, 3, h, rows]
                    if f == 3:
                        total = total + aux[4, h, rows]
                    else:
                        total = total * aux[5, h, rows]
                    self.tend[j, f, h, rows] = total
                    self.base[j, f, h, rows] = near

    def quadrature(self, begin, end):
        n, points, table = self.geo.nodes, self.points, self.table

        def body(t, _):
            rows = pl.ds(pl.multiple_of(t * 8, 8), 8)
            inside = self.mask[rows]
            for f in range(4):
                scale = [inside * (1.0 / (1.0 + 6.0 * points[m] * diffusion[f])) for m in range(n)]
                for h in range(2):
                    slopes = [self.tend[j, f, h, rows] for j in range(n)]
                    begun = self.aux[f, h, rows]
                    for m in range(n):
                        c = points[m] * diffusion[f]
                        total = begun + (6.0 * c) * self.field[m, f, h, rows]
                        for j in range(n):
                            total = total + table[m][j] * slopes[j]
                        total = total * scale[m]
                        self.first[m, f, h, rows] = total
                        self.base[m, f, h, rows] = total - (c * scale[m]) * self.base[m, f, h, rows]
            return 0

        lax.fori_loop(begin // 8, end // 8, body, 0)

    def weights(self, m):
        return [pick(m, [p * d / (1.0 + 6.0 * p * d) for p in self.points]) for d in diffusion]

    def relax_rows(self, source, target, m, f, r, weight, to):
        stride = self.geo.stride
        minus, plus = lane_sides(source[m, f, 0, pl.ds(r, 8)], source[m, f, 1, pl.ds(r, 8)])
        for h in range(2):
            near = (
                (source[m, f, h, pl.ds(r + stride, 8)] + source[m, f, h, pl.ds(r - stride, 8)])
                + (source[m, f, h, pl.ds(r + 1, 8)] + source[m, f, h, pl.ds(r - 1, 8)])
                + (plus[h] + minus[h])
            )
            target[m, f, h, pl.ds(to, 8)] = self.base[m, f, h, pl.ds(r, 8)] + weight * near

    def relax(self, source, target, m, begin, end):
        weight = self.weights(m)
        for r in range(begin, end, 8):
            inside = self.mask[pl.ds(r, 8)]
            for f in range(4):
                self.relax_rows(source, target, m, f, r, inside * weight[f], r)


def each_node(count, body):
    def step(i, _):
        body(i)
        return 0

    lax.fori_loop(0, count, step, 0)


def by_side(odd, body):
    for upper in (False, True):
        pl.when(odd == int(upper))(functools.partial(body, upper))


def start_kernel(geo, opening, tiles, points, table, *refs):
    n, low, side = geo.nodes, geo.low, geo.side
    me, tile = lax.axis_index("node"), lax.axis_index("space")
    odd = tile % 2
    near, far = halo_rows(geo, odd)
    near_from, _ = send_rows(geo, 1 - odd)
    own_rows, near_rows, far_rows = pl.ds(low, geo.rows), pl.ds(near, side), pl.ds(far, side)
    pairs = []
    if opening:
        aux_ref, near0_ref, far0_ref, own0_ref, *rest, aux, mask, field, tend, base, first, sems = refs
        pairs = [(aux_ref, aux.at[:, :, own_rows]), (near0_ref.at[pl.ds(4, 6)], aux.at[:, :, near_rows])]
        fars = []
        for k in range(n):
            sources = own0_ref, near0_ref.at[pl.ds(0, 4)]
            if k:
                own_ref, near_ref, *rest = rest
                sources = own_ref, near_ref.at[:, :, pl.ds(near_from, side)]
            if 0 < k < n - 1:
                far_ref, *rest = rest
                fars.append(far_ref)
            pairs += zip(sources, [field.at[me ^ k, :, :, rows] for rows in (own_rows, near_rows)])
    else:
        aux, mask, own_ref, near_ref, field, tend, base, first, sems = refs
        for k in range(n):
            pairs += [(own_ref.at[k], field.at[k, :, :, own_rows]), (near_ref.at[k], field.at[k, :, :, near_rows])]
    copies = [pltpu.make_async_copy(source, target, sems.at[i]) for i, (source, target) in enumerate(pairs)]
    for copy in copies:
        copy.start()

    field[:, :, :, far_rows] = jnp.zeros((n, 4, 2, side, LANES), jnp.float32)
    if opening:
        aux[:, :, far_rows] = jnp.zeros((6, 2, side, LANES), jnp.float32)
        mask[...] = jnp.zeros(mask.shape, jnp.float32)
        for q in range(-JACOBI, geo.planes + JACOBI):
            there = jnp.float32(1.0)
            if q < 0:
                there = jnp.where(tile > 0, 1.0, 0.0)
            if q >= geo.planes:
                there = jnp.where(tile < tiles - 1, 1.0, 0.0)
            at = low + q * geo.stride
            mask[at : at + geo.window] = jnp.full((geo.window, LANES), there, jnp.float32)

        def unpack_far(upper, lowest):
            for f, h, cuts, row in geo.mixed():
                place(geo, cuts, upper, lowest, far0_ref, aux.at[f - 4, h] if f >= 4 else field.at[me, f, h], row)
            for k in range(1, n - 1):
                for f, h, cuts, row in geo.fields(False)[0]:
                    place(geo, cuts, upper, lowest, fars[k - 1], field.at[me ^ k, f, h], row)

        each_place(me, odd, unpack_far)
        for copy in copies[:2]:
            copy.wait()

    steps = Steps(geo, points, table, aux, mask, field, tend, base, first)
    shift = 2 if opening else 0

    def arrive(k, j):
        for i, rows in enumerate((own_rows, near_rows)):
            part = field.at[j, :, :, rows]
            pltpu.make_async_copy(part, part, sems.at[shift + 2 * k + i]).wait()

    if opening:

        def whole(k):
            arrive(k, me ^ k)
            steps.slopes(me ^ k, *geo.span(JACOBI - 1))

        each_node(n - 1, whole)
        arrive(n - 1, me ^ (n - 1))

    def early(upper):
        rows, second = geo.early(upper)
        if opening:
            steps.slopes(me ^ (n - 1), *rows)
        else:

            def part(k):
                arrive(k, k)
                steps.slopes(k, *rows)

            each_node(n, part)
        steps.quadrature(*rows)
        each_node(n, lambda m: steps.relax(first, tend, m, *second))

    by_side(odd, early)


def finish_kernel(geo, opening, points, table, aux, mask, *refs):
    n, stride, low, side = geo.nodes, geo.stride, geo.low, geo.side
    me, odd = lax.axis_index("node"), lax.axis_index("space") % 2
    far_ref = refs[4]
    field, tend, base, first, *outs, sems = refs[5:]
    steps = Steps(geo, points, table, aux, mask, field, tend, base, first)

    def unpack_far(upper, lowest):
        for f, h, cuts, row in geo.fields(not opening)[0]:
            if opening:
                place(geo, cuts, upper, lowest, far_ref, field.at[me ^ (n - 1), f, h], row)
            else:
                for k in range(n):
                    place(geo, cuts, upper, lowest, far_ref.at[k], field.at[k, f, h], row)

    each_place(me, odd, unpack_far)

    def late(upper):
        rows, second = geo.late(upper)
        if opening:
            steps.slopes(me ^ (n - 1), *rows)
        else:
            each_node(n, lambda j: steps.slopes(j, *rows))
        steps.quadrature(*rows)
        each_node(n, lambda m: steps.relax(first, tend, m, *second))

    by_side(odd, late)

    if opening:
        out_ref, near_out, far_out = outs
        near_row = send_rows(geo, odd)[0]

        def results(m):
            copies = []
            for i, (row, count, ref) in enumerate(((near_row, side, near_out), (0, geo.rows, out_ref))):
                part = first.at[m, :, :, pl.ds(pl.multiple_of(low + row, 8), count)]
                copies.append(pltpu.make_async_copy(part, ref.at[m], sems.at[2 * m + i]))
            return copies

        def third(m):
            steps.relax(tend, first, m, *geo.span(0))
            for copy in results(m):
                copy.start()

            def pack_far(upper, lowest):
                for f, h, cuts, row in geo.fields(True)[0]:
                    trim(geo, cuts, upper, lowest, first.at[m, f, h], low, far_out.at[m], row)

            each_place(me, odd, pack_far)

        each_node(n, third)
        for m in range(n):
            for copy in results(m):
                copy.wait()
        return

    done = pl.ds(0, geo.planes * geo.back)
    for start in sorted({a - b for a, b in zip(geo.first, geo.offset)}):
        hit = [p for p in range(n) if geo.first[p] - geo.offset[p] == start]
        chosen = functools.reduce(jnp.logical_or, [me == p for p in hit])

        @pl.when(chosen)
        def _():
            def third(i):
                k = n - 1 - i
                m = me ^ k
                weight = steps.weights(m)
                for x in range(geo.planes):
                    for o in [*range(0, geo.back - 8, 8), geo.back - 8]:
                        for f in range(4):
                            r = low + x * stride + start + o
                            steps.relax_rows(tend, first, m, f, r, weight[f], x * geo.back + o)
                for other in range(n):

                    @pl.when(k == other)
                    def _():
                        pltpu.make_async_copy(first.at[m, :, :, done], outs[other], sems.at[other]).start()

            each_node(n, third)

    for k in range(n):
        pltpu.make_async_copy(first.at[me ^ k, :, :, done], outs[k], sems.at[k]).wait()


def unpack_kernel(geo, *refs):
    ins, (out_ref, whole, sems) = refs[: geo.nodes], refs[geo.nodes :]
    me = lax.axis_index("node")
    copies = [pltpu.make_async_copy(whole.at[f], out_ref.at[0, f], sems.at[f]) for f in range(4)]
    for f in range(4):
        for k in range(geo.nodes):
            for p in range(geo.nodes):

                @pl.when(me == p ^ k)
                def _():
                    rows = slice(geo.first[p], geo.first[p] + geo.count[p])
                    for x in range(geo.planes):
                        for h in range(2):
                            at = x * geo.back
                            whole[f, x, rows, h * LANES : (h + 1) * LANES] = ins[k][f, h, at : at + geo.count[p]]

        copies[f].start()
    for copy in copies:
        copy.wait()


def on_device(start, guess, heat_mask, solid_mask):
    n = lax.axis_size("node")
    tiles = lax.axis_size("space")
    planes, depth, width = guess.shape[2:]
    assert width == 2 * LANES and tiles % 2 == 0 and n & (n - 1) == 0
    geo = Geometry(n, planes, depth)
    points_list, table_list = radau_tables(n)
    table = [[float(np.float32(v)) for v in row] for row in table_list]
    points = [float(np.float32(v)) for v in points_list]
    f32 = jnp.float32
    vmem, free = pl.BlockSpec(memory_space=pltpu.VMEM), pl.BlockSpec(memory_space=pl.ANY)

    def call(kernel, name, outs, out_specs, ins, in_specs, scratch, copies, aliases={}):
        held = list(scratch)
        semaphores = [pltpu.SemaphoreType.DMA((copies,))] if copies else []
        return pl.pallas_call(
            kernel, name=name,
            out_shape=[jax.ShapeDtypeStruct(shape, f32) for shape in outs], in_specs=in_specs, out_specs=out_specs,
            input_output_aliases=aliases,
            scratch_shapes=[a if hasattr(a, "memory_space") else pltpu.VMEM(a, f32) for a in scratch] + semaphores,
            compiler_params=pltpu.CompilerParams(vmem_limit_bytes=VMEM_SLACK + 4 * sum(map(size_of, held))),
        )(*ins)

    def across(k, value):
        return lax.ppermute(value, "node", [(i, i ^ k) for i in range(n)])

    chip = [(i, i ^ 1) for i in range(tiles)]
    links = [(i, i + 1) for i in range(1, tiles - 1, 2)] + [(i + 1, i) for i in range(1, tiles - 1, 2)]

    def beside(near, far):
        return lax.ppermute(near, "space", chip), lax.ppermute(far, "space", links)

    piece = (4, 2, geo.rows, LANES)
    sends = call(
        functools.partial(pack_kernel, geo), "pack", [piece] * (n - 1), [free] * (n - 1), (guess,), [vmem],
        [(n,) + piece], n - 1,
    )
    geo.mixed()
    masks = pltpu.VMEM(heat_mask.shape, jnp.int32)
    own, aux, near, far = call(
        functools.partial(pack_own_kernel, geo), "pack_own",
        [piece, (6,) + piece[1:], (10, 2, geo.side, LANES), (geo.mixed_rows, LANES)], [free, free, free, vmem],
        (guess, start, heat_mask, solid_mask), [pl.BlockSpec(memory_space=pltpu.HBM)] * 4,
        [guess.shape, start.shape, masks, masks, (10,) + piece[1:]], 4,
    )
    near0, far0 = beside(near, far)

    owns = {0: own}
    wave = []
    for hops in range(1, n.bit_length()):
        group = [k for k in range(1, n) if k.bit_count() == hops]
        gated = lax.optimization_barrier([sends[k - 1] for k in group] + wave)
        wave = [across(k, value) for k, value in zip(group, gated)]
        owns.update(zip(group, wave))
    pieces, specs = [own], [free]
    for k in range(1, n):
        (far,) = call(
            functools.partial(trim_kernel, geo), "trim", [(geo.fields(False)[1], LANES)], [vmem],
            (owns[k],), [vmem], [], 0,
        )
        held = owns[k]
        if k == n - 1:
            held, far = lax.optimization_barrier((held, far))
        near, far = beside(held, far)
        pieces += [owns[k], near]
        specs += [free, free]
        if k < n - 1:
            pieces.append(far)
            specs.append(vmem)

    big = (n, 4, 2, geo.total, LANES)
    state, kept = [big] * 4, [(6, 2, geo.total, LANES), (geo.total, LANES)]
    sent = (n, geo.fields(True)[1], LANES)
    aux, mask, *held = call(
        functools.partial(start_kernel, geo, True, tiles, points, table), "opening_start", kept + state, [vmem] * 6,
        (aux, near0, far0, *pieces), [free, free, vmem, *specs], [], 2 + 2 * n,
    )
    aliases = {2 + i: i for i in range(4)}
    own, near, far = call(
        functools.partial(finish_kernel, geo, True, points, table), "opening_finish",
        state + [(n,) + piece, (n, 4, 2, geo.side, LANES), sent], [vmem] * 4 + [free, free, vmem],
        (aux, mask, *held, far), [vmem] * 7, [], 2 * n, aliases,
    )[4:]
    near, far = beside(near, far)
    held = call(
        functools.partial(start_kernel, geo, False, tiles, points, table), "closing_start", state, [vmem] * 4,
        (aux, mask, own, near), [vmem, vmem, free, free], [], 2 * n,
    )
    outs = call(
        functools.partial(finish_kernel, geo, False, points, table), "closing_finish",
        state + [(4, 2, planes * geo.back, LANES)] * n, [vmem] * 4 + [free] * n,
        (aux, mask, *held, far), [vmem] * 7, [], n, aliases,
    )[4:]
    outs = [across(k, outs[k]) if k else outs[k] for k in range(n)]
    (result,) = call(
        functools.partial(unpack_kernel, geo), "unpack", [(1, 4, planes, depth, width)], [free], outs, [vmem] * n,
        [(4, planes, depth, width)], 4,
    )
    return result


def solution(mesh):
    in_specs = (
        P(None, "space", None, None),
        P("node", None, "space", None, None),
        P("space", None, None),
        P("space", None, None),
    )
    out_specs = P("node", None, "space", None, None)
    return jax.shard_map(
        on_device, mesh=mesh, in_specs=in_specs, out_specs=out_specs, check_vma=False
    )
```

```python
import functools
import math

import jax
import jax.numpy as jnp
import numpy as np
from jax import lax
from jax.experimental import pallas as pl
from jax.experimental.pallas import tpu as pltpu
from jax.sharding import PartitionSpec as P

SWEEPS = 2
JACOBI = 3
LANES = 128
VMEM_SLACK = 2 << 20

advect_rate = 0.25
buoyancy = 0.5
heating = 1.0
diffusion = (0.5, 0.5, 0.5, 0.35)


def legendre_value(order, place):
    previous = 1.0
    current = place
    for degree in range(1, order):
        following = ((2 * degree + 1) * place * current - degree * previous) / (degree + 1)
        previous = current
        current = following
    return current


def radau_tables(count):

    def radau_poly(place):
        return legendre_value(count, place) - legendre_value(count - 1, place)

    samples = 4000 * count
    roots_found = []
    left_end = -1.0
    left_value = radau_poly(left_end)
    for index in range(1, samples + 1):
        right_end = -1.0 + (2.0 - 1e-07) * index / samples
        right_value = radau_poly(right_end)
        if left_value * right_value < 0.0:
            low_end = left_end
            high_end = right_end
            low_value = left_value
            for repeat in range(200):
                middle = 0.5 * (low_end + high_end)
                middle_value = radau_poly(middle)
                if low_value * middle_value <= 0.0:
                    high_end = middle
                else:
                    low_end = middle
                    low_value = middle_value
            roots_found.append(0.5 * (low_end + high_end))
        left_end = right_end
        left_value = right_value
    points = [(value + 1.0) / 2.0 for value in roots_found[: count - 1]] + [1.0]
    table = []
    for row in range(count):
        table.append([0.0] * count)
    for column in range(count):
        coefficients = [1.0]
        for other in range(count):
            if other == column:
                continue
            scale = 1.0 / (points[column] - points[other])
            widened = [0.0] * (len(coefficients) + 1)
            for index in range(len(coefficients)):
                widened[index + 1] += coefficients[index] * scale
                widened[index] -= points[other] * coefficients[index] * scale
            coefficients = widened
        for row in range(count):
            total = 0.0
            for index in range(len(coefficients)):
                total += coefficients[index] * points[row] ** (index + 1) / (index + 1)
            table[row][column] = total
    return (points, table)


def size_of(shape):
    return math.prod(getattr(shape, "shape", shape))


def round_up(value, step):
    return -(-value // step) * step


class Geometry:
    def __init__(self, nodes, planes, depth):
        overlap = SWEEPS * JACOBI if nodes > 1 else 0
        self.nodes, self.planes, self.depth = nodes, planes, depth
        self.window = -(-(depth + 2 * overlap * (nodes - 1)) // nodes)
        step = self.window - 2 * overlap
        assert step > 0 and planes >= JACOBI
        self.offset = [min(p * step, depth - self.window) for p in range(nodes)]
        first = [0] + [p * step + overlap for p in range(1, nodes)]
        last = first[1:] + [depth]
        self.first, self.count = first, [b - a for a, b in zip(first, last)]
        self.stride = self.window + 1
        while (planes * self.stride) % 8:
            self.stride += 1
        self.rows = planes * self.stride
        self.side = round_up(JACOBI * self.stride, 8)
        self.low = 8 + self.side
        self.total = self.low + self.rows + self.side + 8
        self.back = max(self.count)
        while (planes * self.back) % 8:
            self.back += 1

    def trims(self, closing, reach):
        packed, cuts = 0, []
        for d in range(1, reach + 1):
            cut = closing * JACOBI + d
            cuts.append((d, cut, packed, self.window - cut))
            packed += self.window - cut
        return cuts, packed

    def mixed(self):
        row, parts = 0, []
        for f in range(10):
            cuts, count = self.trims(False, JACOBI if f < 4 else JACOBI - 1)
            for h in range(2):
                parts.append((f, h, cuts, row))
                row += count
        self.mixed_rows = round_up(row, 8)
        return parts

    def fields(self, closing):
        cuts, count = self.trims(closing, JACOBI)
        return [(f, h, cuts, (2 * f + h) * count) for f in range(4) for h in range(2)], round_up(8 * count, 8)

    def span(self, reach):
        begin = (self.low - reach * self.stride) // 8 * 8
        end = round_up(self.low + (self.planes + reach) * self.stride, 8)
        assert begin - self.stride >= 0 and end + self.stride <= self.total
        return begin, end

    def early(self, upper):
        begin, end = self.span(JACOBI - 1)
        second_begin, second_end = self.span(JACOBI - 2)
        if upper:
            end = (self.low + (self.planes - 1) * self.stride) // 8 * 8
            second_end = (end - self.stride) // 8 * 8
        else:
            begin = round_up(self.low + self.stride, 8)
            second_begin = round_up(begin + self.stride, 8)
        return (begin, end), (second_begin, second_end)

    def late(self, upper):
        rest = []
        for whole, part in zip((self.span(JACOBI - 1), self.span(JACOBI - 2)), self.early(upper)):
            rest.append((part[1], whole[1]) if upper else (whole[0], part[0]))
        return rest


def copy_all(pairs, sems):
    copies = [pltpu.make_async_copy(source, target, sems.at[i]) for i, (source, target) in enumerate(pairs)]
    for copy in copies:
        copy.start()
    for copy in copies:
        copy.wait()


def pack_kernel(geo, guess_ref, *refs):
    *outs, windows, sems = refs
    me = lax.axis_index("node")
    blank = jnp.zeros((geo.stride - geo.window, LANES), jnp.float32)
    for p in range(geo.nodes):
        for f in range(4):
            for x in range(geo.planes):
                for h in range(2):
                    at = x * geo.stride
                    windows[p, f, h, at : at + geo.window] = guess_ref[
                        0, f, x, geo.offset[p] : geo.offset[p] + geo.window, h * LANES : (h + 1) * LANES
                    ]
                    windows[p, f, h, at + geo.window : at + geo.stride] = blank
    copy_all([(windows.at[me ^ k], outs[k - 1]) for k in range(1, geo.nodes)], sems)


def send_rows(geo, odd):
    far = geo.rows - geo.side
    return pl.multiple_of(far * (1 - odd), 8), pl.multiple_of(far * odd, 8)


def each_place(me, odd, body):
    for upper in (False, True):
        for lowest in (False, True):
            pl.when((odd == int(upper)) & ((me == 0) == lowest))(functools.partial(body, upper, lowest))


def trim(geo, cuts, upper, lowest, source, at, target, to=0):
    for d, cut, packed, count in cuts:
        plane = geo.planes - d if upper else d - 1
        row = at + plane * geo.stride + (0 if lowest else cut)
        target[to + packed : to + packed + count] = source[row : row + count]


def place(geo, cuts, upper, lowest, source, target, start=0):
    for d, cut, packed, count in cuts:
        plane = geo.planes - 1 + d if upper else -d
        row = geo.low + plane * geo.stride + (0 if lowest else cut)
        target[row : row + count] = source[start + packed : start + packed + count]


def trim_kernel(geo, own_ref, far_ref):
    def body(upper, lowest):
        for f, h, cuts, row in geo.fields(False)[0]:
            trim(geo, cuts, upper, lowest, own_ref.at[f, h], 0, far_ref, row)

    each_place(lax.axis_index("node"), lax.axis_index("space") % 2, body)


def halo_rows(geo, odd):
    below, above = geo.low - geo.side, geo.low + geo.rows
    return (
        pl.multiple_of(above + (below - above) * odd, 8),
        pl.multiple_of(below + (above - below) * odd, 8),
    )


def pack_own_kernel(
    geo, guess_hbm, start_hbm, heat_hbm, solid_hbm, own_ref, aux_ref, near_ref, far_ref,
    guess_ref, start_ref, heat_ref, solid_ref, packed, sems,
):
    me, odd = lax.axis_index("node"), lax.axis_index("space") % 2
    copy_all(
        [(guess_hbm, guess_ref), (start_hbm, start_ref), (heat_hbm, heat_ref), (solid_hbm, solid_ref)], sems
    )
    blank = jnp.zeros((geo.stride - geo.window, LANES), jnp.float32)
    for p in range(geo.nodes):

        @pl.when(me == p)
        def _():
            rows = slice(geo.offset[p], geo.offset[p] + geo.window)
            for x in range(geo.planes):
                for h in range(2):
                    at = x * geo.stride
                    lanes = slice(h * LANES, (h + 1) * LANES)
                    for f in range(4):
                        packed[f, h, at : at + geo.window] = guess_ref[0, f, x, rows, lanes]
                        packed[4 + f, h, at : at + geo.window] = start_ref[f, x, rows, lanes]
                    packed[8, h, at : at + geo.window] = heating * heat_ref[x, rows, lanes].astype(jnp.float32)
                    packed[9, h, at : at + geo.window] = 1.0 - solid_ref[x, rows, lanes].astype(jnp.float32)
                    for f in range(10):
                        packed[f, h, at + geo.window : at + geo.stride] = blank

    near, far = send_rows(geo, odd)
    copies = [
        pltpu.make_async_copy(packed.at[:, :, pl.ds(near, geo.side)], near_ref, sems.at[0]),
        pltpu.make_async_copy(packed.at[pl.ds(0, 4)], own_ref, sems.at[1]),
        pltpu.make_async_copy(packed.at[pl.ds(4, 6)], aux_ref, sems.at[2]),
    ]
    for copy in copies:
        copy.start()

    def body(upper, lowest):
        for f, h, cuts, row in geo.mixed():
            trim(geo, cuts, upper, lowest, packed.at[f, h], 0, far_ref, row)

    each_place(me, odd, body)
    for copy in copies:
        copy.wait()


def pick(index, values):
    chosen = jnp.float32(values[-1])
    for i in reversed(range(len(values) - 1)):
        chosen = jnp.where(index == i, jnp.float32(values[i]), chosen)
    return chosen


def lane_sides(a, b):
    lane = lax.broadcasted_iota(jnp.int32, (8, LANES), 1)
    is_first, is_last = lane == 0, lane == LANES - 1
    ra, rb = pltpu.roll(a, 1, 1), pltpu.roll(b, 1, 1)
    la, lb = pltpu.roll(a, LANES - 1, 1), pltpu.roll(b, LANES - 1, 1)
    minus = (jnp.where(is_first, 0.0, ra), jnp.where(is_first, ra, rb))
    plus = (jnp.where(is_last, lb, la), jnp.where(is_last, 0.0, lb))
    return minus, plus


class Steps:
    def __init__(self, geo, points, table, aux, mask, field, tend, base, first):
        self.geo, self.points, self.table = geo, points, table
        self.aux, self.mask, self.field, self.tend, self.base, self.first = aux, mask, field, tend, base, first

    def slopes(self, j, begin, end):
        field, aux, stride = self.field, self.aux, self.geo.stride
        for r in range(begin, end, 8):
            rows = pl.ds(r, 8)
            vel = []
            for h in range(2):
                vel.append([(-0.5 * advect_rate) * field[j, f, h, rows] for f in range(3)])
            for f in range(4):
                centre = [field[j, f, h, rows] for h in range(2)]
                minus, plus = lane_sides(centre[0], centre[1])
                for h in range(2):
                    xp, xm = field[j, f, h, pl.ds(r + stride, 8)], field[j, f, h, pl.ds(r - stride, 8)]
                    zp, zm = field[j, f, h, pl.ds(r + 1, 8)], field[j, f, h, pl.ds(r - 1, 8)]
                    near = (xp + xm) + (zp + zm) + (plus[h] + minus[h])
                    moved = vel[h][0] * (xp - xm) + vel[h][1] * (plus[h] - minus[h]) + vel[h][2] * (zp - zm)
                    total = moved + diffusion[f] * (near - 6.0 * centre[h])
                    if f == 2:
                        total = total + buoyancy * field[j, 3, h, rows]
                    if f == 3:
                        total = total + aux[4, h, rows]
                    else:
                        total = total * aux[5, h, rows]
                    self.tend[j, f, h, rows] = total
                    self.base[j, f, h, rows] = near

    def quadrature(self, begin, end):
        n, points, table = self.geo.nodes, self.points, self.table

        def body(t, _):
            rows = pl.ds(pl.multiple_of(t * 8, 8), 8)
            inside = self.mask[rows]
            for f in range(4):
                scale = [inside * (1.0 / (1.0 + 6.0 * points[m] * diffusion[f])) for m in range(n)]
                for h in range(2):
                    slopes = [self.tend[j, f, h, rows] for j in range(n)]
                    begun = self.aux[f, h, rows]
                    for m in range(n):
                        c = points[m] * diffusion[f]
                        total = begun + (6.0 * c) * self.field[m, f, h, rows]
                        for j in range(n):
                            total = total + table[m][j] * slopes[j]
                        total = total * scale[m]
                        self.first[m, f, h, rows] = total
                        self.base[m, f, h, rows] = total - (c * scale[m]) * self.base[m, f, h, rows]
            return 0

        lax.fori_loop(begin // 8, end // 8, body, 0)

    def weights(self, m):
        return [pick(m, [p * d / (1.0 + 6.0 * p * d) for p in self.points]) for d in diffusion]

    def relax_rows(self, source, target, m, f, r, weight, to):
        stride = self.geo.stride
        minus, plus = lane_sides(source[m, f, 0, pl.ds(r, 8)], source[m, f, 1, pl.ds(r, 8)])
        for h in range(2):
            near = (
                (source[m, f, h, pl.ds(r + stride, 8)] + source[m, f, h, pl.ds(r - stride, 8)])
                + (source[m, f, h, pl.ds(r + 1, 8)] + source[m, f, h, pl.ds(r - 1, 8)])
                + (plus[h] + minus[h])
            )
            target[f, h, pl.ds(to, 8)] = self.base[m, f, h, pl.ds(r, 8)] + weight * near

    def relax(self, source, target, m, begin, end):
        weight = self.weights(m)
        for r in range(begin, end, 8):
            inside = self.mask[pl.ds(r, 8)]
            for f in range(4):
                self.relax_rows(source, target.at[m], m, f, r, inside * weight[f], r)


def each_node(count, body):
    def step(i, _):
        body(i)
        return 0

    lax.fori_loop(0, count, step, 0)


def by_side(odd, body):
    for upper in (False, True):
        pl.when(odd == int(upper))(functools.partial(body, upper))


def start_kernel(geo, opening, tiles, points, table, *refs):
    n, low, side = geo.nodes, geo.low, geo.side
    me, tile = lax.axis_index("node"), lax.axis_index("space")
    odd = tile % 2
    near, far = halo_rows(geo, odd)
    near_from, _ = send_rows(geo, 1 - odd)
    own_rows, near_rows, far_rows = pl.ds(low, geo.rows), pl.ds(near, side), pl.ds(far, side)
    pairs = []
    if opening:
        aux_ref, near0_ref, far0_ref, own0_ref, *rest, aux, mask, field, tend, base, first, sems = refs
        pairs = [(aux_ref, aux.at[:, :, own_rows]), (near0_ref.at[pl.ds(4, 6)], aux.at[:, :, near_rows])]
        fars = []
        for k in range(n):
            sources = own0_ref, near0_ref.at[pl.ds(0, 4)]
            if k:
                own_ref, near_ref, *rest = rest
                sources = own_ref, near_ref.at[:, :, pl.ds(near_from, side)]
            if 0 < k < n - 1:
                far_ref, *rest = rest
                fars.append(far_ref)
            pairs += zip(sources, [field.at[me ^ k, :, :, rows] for rows in (own_rows, near_rows)])
    else:
        aux, mask, own_ref, near_ref, field, tend, base, first, sems = refs
        for k in range(n):
            pairs += [(own_ref.at[k], field.at[k, :, :, own_rows]), (near_ref.at[k], field.at[k, :, :, near_rows])]
    copies = [pltpu.make_async_copy(source, target, sems.at[i]) for i, (source, target) in enumerate(pairs)]
    for copy in copies:
        copy.start()

    field[:, :, :, far_rows] = jnp.zeros((n, 4, 2, side, LANES), jnp.float32)
    if opening:
        aux[:, :, far_rows] = jnp.zeros((6, 2, side, LANES), jnp.float32)
        mask[...] = jnp.zeros(mask.shape, jnp.float32)
        for q in range(-JACOBI, geo.planes + JACOBI):
            there = jnp.float32(1.0)
            if q < 0:
                there = jnp.where(tile > 0, 1.0, 0.0)
            if q >= geo.planes:
                there = jnp.where(tile < tiles - 1, 1.0, 0.0)
            at = low + q * geo.stride
            mask[at : at + geo.window] = jnp.full((geo.window, LANES), there, jnp.float32)

        def unpack_far(upper, lowest):
            for f, h, cuts, row in geo.mixed():
                place(geo, cuts, upper, lowest, far0_ref, aux.at[f - 4, h] if f >= 4 else field.at[me, f, h], row)
            for k in range(1, n - 1):
                for f, h, cuts, row in geo.fields(False)[0]:
                    place(geo, cuts, upper, lowest, fars[k - 1], field.at[me ^ k, f, h], row)

        each_place(me, odd, unpack_far)
        for copy in copies[:2]:
            copy.wait()

    steps = Steps(geo, points, table, aux, mask, field, tend, base, first)
    shift = 2 if opening else 0

    def arrive(k, j):
        for i, rows in enumerate((own_rows, near_rows)):
            part = field.at[j, :, :, rows]
            pltpu.make_async_copy(part, part, sems.at[shift + 2 * k + i]).wait()

    if opening:

        def whole(k):
            arrive(k, me ^ k)
            steps.slopes(me ^ k, *geo.span(JACOBI - 1))

        each_node(n - 1, whole)
        arrive(n - 1, me ^ (n - 1))

    def early(upper):
        rows, second = geo.early(upper)
        if opening:
            steps.slopes(me ^ (n - 1), *rows)
        else:

            def part(k):
                arrive(k, k)
                steps.slopes(k, *rows)

            each_node(n, part)
        steps.quadrature(*rows)
        each_node(n, lambda m: steps.relax(first, tend, m, *second))

    by_side(odd, early)


def finish_kernel(geo, opening, points, table, aux, mask, *refs):
    n, stride, low, side = geo.nodes, geo.stride, geo.low, geo.side
    me, odd = lax.axis_index("node"), lax.axis_index("space") % 2
    far_ref = refs[4]
    field, tend, base, first, *outs = refs[5:]
    steps = Steps(geo, points, table, aux, mask, field, tend, base, first)

    def unpack_far(upper, lowest):
        for f, h, cuts, row in geo.fields(not opening)[0]:
            if opening:
                place(geo, cuts, upper, lowest, far_ref, field.at[me ^ (n - 1), f, h], row)
            else:
                for k in range(n):
                    place(geo, cuts, upper, lowest, far_ref.at[k], field.at[k, f, h], row)

    each_place(me, odd, unpack_far)

    def late(upper):
        rows, second = geo.late(upper)
        if opening:
            steps.slopes(me ^ (n - 1), *rows)
        else:
            each_node(n, lambda j: steps.slopes(j, *rows))
        steps.quadrature(*rows)
        each_node(n, lambda m: steps.relax(first, tend, m, *second))

    by_side(odd, late)

    if opening:
        out_ref, near_out, far_out, sems = outs
        near_row = send_rows(geo, odd)[0]

        def results(m):
            copies = []
            for i, (row, count, ref) in enumerate(((near_row, side, near_out), (0, geo.rows, out_ref))):
                part = first.at[m, :, :, pl.ds(pl.multiple_of(low + row, 8), count)]
                copies.append(pltpu.make_async_copy(part, ref.at[m], sems.at[2 * m + i]))
            return copies

        def third(m):
            steps.relax(tend, first, m, *geo.span(0))
            for copy in results(m):
                copy.start()

            def pack_far(upper, lowest):
                for f, h, cuts, row in geo.fields(True)[0]:
                    trim(geo, cuts, upper, lowest, first.at[m, f, h], low, far_out.at[m], row)

            each_place(me, odd, pack_far)

        each_node(n, third)
        for m in range(n):
            for copy in results(m):
                copy.wait()
        return

    for start in sorted({a - b for a, b in zip(geo.first, geo.offset)}):
        hit = [p for p in range(n) if geo.first[p] - geo.offset[p] == start]
        chosen = functools.reduce(jnp.logical_or, [me == p for p in hit])

        @pl.when(chosen)
        def _():
            for k in range(n):
                m = me ^ k
                weight = steps.weights(m)
                for x in range(geo.planes):
                    for o in [*range(0, geo.back - 8, 8), geo.back - 8]:
                        for f in range(4):
                            r = low + x * stride + start + o
                            steps.relax_rows(tend, outs[k], m, f, r, weight[f], x * geo.back + o)


def unpack_kernel(geo, *refs):
    ins, (out_ref, whole, sems) = refs[: geo.nodes], refs[geo.nodes :]
    me = lax.axis_index("node")
    copies = [pltpu.make_async_copy(whole.at[f], out_ref.at[0, f], sems.at[f]) for f in range(4)]
    for f in range(4):
        for k in range(geo.nodes):
            for p in range(geo.nodes):

                @pl.when(me == p ^ k)
                def _():
                    rows = slice(geo.first[p], geo.first[p] + geo.count[p])
                    for x in range(geo.planes):
                        for h in range(2):
                            at = x * geo.back
                            whole[f, x, rows, h * LANES : (h + 1) * LANES] = ins[k][f, h, at : at + geo.count[p]]

        copies[f].start()
    for copy in copies:
        copy.wait()


def on_device(start, guess, heat_mask, solid_mask):
    n = lax.axis_size("node")
    tiles = lax.axis_size("space")
    planes, depth, width = guess.shape[2:]
    assert width == 2 * LANES and tiles % 2 == 0 and n & (n - 1) == 0
    geo = Geometry(n, planes, depth)
    points_list, table_list = radau_tables(n)
    table = [[float(np.float32(v)) for v in row] for row in table_list]
    points = [float(np.float32(v)) for v in points_list]
    f32 = jnp.float32
    vmem, free = pl.BlockSpec(memory_space=pltpu.VMEM), pl.BlockSpec(memory_space=pl.ANY)

    def call(kernel, name, outs, out_specs, ins, in_specs, scratch, copies, aliases={}):
        held = list(scratch)
        semaphores = [pltpu.SemaphoreType.DMA((copies,))] if copies else []
        return pl.pallas_call(
            kernel, name=name,
            out_shape=[jax.ShapeDtypeStruct(shape, f32) for shape in outs], in_specs=in_specs, out_specs=out_specs,
            input_output_aliases=aliases,
            scratch_shapes=[a if hasattr(a, "memory_space") else pltpu.VMEM(a, f32) for a in scratch] + semaphores,
            compiler_params=pltpu.CompilerParams(vmem_limit_bytes=VMEM_SLACK + 4 * sum(map(size_of, held))),
        )(*ins)

    def across(k, value):
        return lax.ppermute(value, "node", [(i, i ^ k) for i in range(n)])

    chip = [(i, i ^ 1) for i in range(tiles)]
    links = [(i, i + 1) for i in range(1, tiles - 1, 2)] + [(i + 1, i) for i in range(1, tiles - 1, 2)]

    def beside(near, far):
        return lax.ppermute(near, "space", chip), lax.ppermute(far, "space", links)

    piece = (4, 2, geo.rows, LANES)
    sends = call(
        functools.partial(pack_kernel, geo), "pack", [piece] * (n - 1), [free] * (n - 1), (guess,), [vmem],
        [(n,) + piece], n - 1,
    )
    geo.mixed()
    masks = pltpu.VMEM(heat_mask.shape, jnp.int32)
    own, aux, near, far = call(
        functools.partial(pack_own_kernel, geo), "pack_own",
        [piece, (6,) + piece[1:], (10, 2, geo.side, LANES), (geo.mixed_rows, LANES)], [free, free, free, vmem],
        (guess, start, heat_mask, solid_mask), [pl.BlockSpec(memory_space=pltpu.HBM)] * 4,
        [guess.shape, start.shape, masks, masks, (10,) + piece[1:]], 4,
    )
    near0, far0 = beside(near, far)

    owns = {0: own}
    wave = []
    for hops in range(1, n.bit_length()):
        group = [k for k in range(1, n) if k.bit_count() == hops]
        gated = lax.optimization_barrier([sends[k - 1] for k in group] + wave)
        wave = [across(k, value) for k, value in zip(group, gated)]
        owns.update(zip(group, wave))
    pieces, specs = [own], [free]
    for k in range(1, n):
        (far,) = call(
            functools.partial(trim_kernel, geo), "trim", [(geo.fields(False)[1], LANES)], [vmem],
            (owns[k],), [vmem], [], 0,
        )
        held = owns[k]
        if k == n - 1:
            held, far = lax.optimization_barrier((held, far))
        near, far = beside(held, far)
        pieces += [owns[k], near]
        specs += [free, free]
        if k < n - 1:
            pieces.append(far)
            specs.append(vmem)

    big = (n, 4, 2, geo.total, LANES)
    state, kept = [big] * 4, [(6, 2, geo.total, LANES), (geo.total, LANES)]
    sent = (n, geo.fields(True)[1], LANES)
    aux, mask, *held = call(
        functools.partial(start_kernel, geo, True, tiles, points, table), "opening_start", kept + state, [vmem] * 6,
        (aux, near0, far0, *pieces), [free, free, vmem, *specs], [], 2 + 2 * n,
    )
    aliases = {2 + i: i for i in range(4)}
    own, near, far = call(
        functools.partial(finish_kernel, geo, True, points, table), "opening_finish",
        state + [(n,) + piece, (n, 4, 2, geo.side, LANES), sent], [vmem] * 4 + [free, free, vmem],
        (aux, mask, *held, far), [vmem] * 7, [], 2 * n, aliases,
    )[4:]
    near, far = beside(near, far)
    held = call(
        functools.partial(start_kernel, geo, False, tiles, points, table), "closing_start", state, [vmem] * 4,
        (aux, mask, own, near), [vmem, vmem, free, free], [], 2 * n,
    )
    outs = call(
        functools.partial(finish_kernel, geo, False, points, table), "closing_finish",
        state + [(4, 2, planes * geo.back, LANES)] * n, [vmem] * (4 + n),
        (aux, mask, *held, far), [vmem] * 7, [], 0, aliases,
    )[4:]
    outs = [across(k, outs[k]) if k else outs[k] for k in range(n)]
    (result,) = call(
        functools.partial(unpack_kernel, geo), "unpack", [(1, 4, planes, depth, width)], [free], outs, [vmem] * n,
        [(4, planes, depth, width)], 4,
    )
    return result


def solution(mesh):
    in_specs = (
        P(None, "space", None, None),
        P("node", None, "space", None, None),
        P("space", None, None),
        P("space", None, None),
    )
    out_specs = P("node", None, "space", None, None)
    return jax.shard_map(
        on_device, mesh=mesh, in_specs=in_specs, out_specs=out_specs, check_vma=False
    )
```
